32 devices in a mesh: groups: 2 (over x), acq: 16 (over z, y, core).
Axes of the slice: x: 2, y: 2, z: 4, core: 2. Of those that a mesh axis runs over, the one named last changes fastest.
Arguments:
- measurements: bfloat16 [128, 2, 16, 12, 256], P(('groups', 'acq')), parts along dimension 0, may hold values from -96 to 96
- tile_order: int32 [32], P('groups'), parts along dimension 0, may hold values from 0 to 15, each once
- steer_phase: float32 [32, 64, 512], P(('groups', 'acq')), parts along dimension 0, may hold values from -3.140625 to 3.140625
- group_ids: int32 [384, 256], P(('groups', 'acq')), parts along dimension 0, may hold values from 0 to 49151, as said below
Outputs:
- elevation_profile: bfloat16 [384, 256, 1024], P(('groups', 'acq')), parts along dimension 0
The draws below stay inside these ranges and needn't reach their ends.
There are 2 independent parts, one for each index of `groups`. The reference program is written for one: setup_inputs(seed, part) draws one part's arguments, and reference() takes and returns one part's arrays. A program takes and returns all parts, laid end to end along the dimension named above; each array names one. Nothing has to cross between parts.
Inputs may be any that keep to these rules, and one draw needn't show every extreme that they name: `tile_order`: each tile of the window appears once. `group_ids`: equal labels mark the pixels of one joint group; the window's rows fall into bands of 3 consecutive rows (fewer at its top, and a band begins at its last row), each band's columns into runs of 3 consecutive columns (fewer at its sides; in the last band a run begins at the last column), and each band-run rectangle is one group; a group's label is the flat index row * 256 + column of its top-left pixel.
All inputs are finite; a program needn't handle non-finite values.
Results may differ from the reference program's by a relative error of at most 0.0054.
Values may be sent and summed in bfloat16 or wider, within the bound.
No kernel may reach another device: no remote copies, remote signals or barrier semaphores. Data moves between devices by JAX's collectives and lax.ppermute only.
A program may use at most 128 MiB of HBM per device.

```python
import math
import jax
import jax.numpy as jnp

M = 64
E = 512
ITERS = 3
TROWS = 12
COLS = 256
TILES = 16
ROWS = 192


def draw_group_ids(key, part):
    base = jax.random.fold_in(key, 11)
    column_key = jax.random.fold_in(base, 5)
    row_phase = (ROWS - 1) % 3
    band_count = ROWS // 3 + 2
    column_phases = jax.random.randint(column_key, (band_count,), 0, 3)
    row_index = jnp.arange(ROWS, dtype=jnp.int32)
    band_index = (row_index - row_phase + 3) // 3
    last_band = (ROWS - 1 - row_phase + 3) // 3
    column_phases = column_phases.at[last_band].set((COLS - 1) % 3)
    row_start = jnp.maximum(0, 3 * band_index - 3 + row_phase)
    phase_of_row = column_phases[band_index]
    column_index = jnp.arange(COLS, dtype=jnp.int32)
    column_band = (column_index[None, :] - phase_of_row[:, None] + 3) // 3
    column_start = jnp.maximum(0, 3 * column_band - 3 + phase_of_row[:, None])
    return (row_start[:, None] * COLS + column_start).astype(jnp.int32)


def shard_levels(key, extent, cuts, least, largest):
    factor_of = 1.0
    for axis_at, blocks in cuts:
        draws = jax.random.uniform(jax.random.fold_in(jax.random.fold_in(key, 6), axis_at), (blocks,), jnp.float32, least / len(cuts), largest / len(cuts))
        factor_of = factor_of * jnp.repeat(jnp.exp(draws), extent[axis_at] // blocks).reshape((-1,) + (1,) * (len(extent) - 1 - axis_at))
    return factor_of


def centred(stream_key, extent, scale, limit, shards=(), kind=jnp.bfloat16):
    values = scale * jax.random.normal(stream_key, extent, jnp.float32)
    if shards:
        values = values * shard_levels(stream_key, extent, shards, -0.22, 0.18)
    return jnp.clip(values, -limit, limit).astype(kind)


def setup_inputs(seed: int = 0, part: int = 0) -> dict:
    splits = jax.random.split(jax.random.key(seed), 5)
    own_keys = jax.random.split(jax.random.fold_in(splits[4], part), 5)
    return {
        "measurements": centred(own_keys[0], (M, 2, TILES, TROWS, COLS), 16.0, 96.0, ((0, 16),)),
        "tile_order": jax.random.permutation(own_keys[1], TILES).astype(jnp.int32),
        "steer_phase": jnp.clip(jax.random.uniform(own_keys[2], (TILES, M, E), jnp.float32, -3.140625, 3.140625), -3.140625, 3.140625),
        "group_ids": draw_group_ids(jax.random.fold_in(jax.random.fold_in(splits[4], part), 71), part),
    }


STEP_SIZE = 0.0625
SHRINK_LEVEL = 3.0

def group_sum(energy, labels):
    padded = jnp.pad(energy, ((2, 2), (2, 2), (0, 0)))
    padded_ids = jnp.pad(labels, 2, constant_values=-1)
    row_sums = jnp.zeros((ROWS + 4, COLS, E), jnp.float32)
    for offset in range(5):
        same = padded_ids[:, offset:offset + COLS] == padded_ids[:, 2:2 + COLS]
        row_sums = row_sums + jnp.where(same[:, :, None], padded[:, offset:offset + COLS], 0.0)
    totals = jnp.zeros((ROWS, COLS, E), jnp.float32)
    for offset in range(5):
        same = padded_ids[offset:offset + ROWS, 2:2 + COLS] == padded_ids[2:2 + ROWS, 2:2 + COLS]
        totals = totals + jnp.where(same[:, :, None], row_sums[offset:offset + ROWS], 0.0)
    return totals

def reference(measurements, tile_order, steer_phase, group_ids):
    places = jnp.zeros((TILES,), jnp.int32).at[tile_order].set(jnp.arange(TILES, dtype=jnp.int32))
    ordered = jnp.take(measurements, places, axis=2)
    pixels = TROWS * COLS
    target_real = ordered[:, 0].reshape(M, TILES, pixels).transpose(1, 0, 2).astype(jnp.float32)
    target_imag = ordered[:, 1].reshape(M, TILES, pixels).transpose(1, 0, 2).astype(jnp.float32)
    norm_scale = 1.0 / math.sqrt(M)
    real_part = (jnp.cos(steer_phase) * norm_scale).astype(jnp.bfloat16).astype(jnp.float32)
    imag_part = (jnp.sin(steer_phase) * norm_scale).astype(jnp.bfloat16).astype(jnp.float32)
    iter_real = jnp.zeros((TILES, pixels, E), jnp.float32)
    iter_imag = jnp.zeros((TILES, pixels, E), jnp.float32)
    for iteration in range(ITERS):
        if iteration == 0:
            resid_real = -target_real
            resid_imag = -target_imag
        else:
            xb_real = iter_real.astype(jnp.bfloat16).astype(jnp.float32)
            xb_imag = iter_imag.astype(jnp.bfloat16).astype(jnp.float32)
            pred_real = jnp.einsum('tme,tpe->tmp', real_part, xb_real) - jnp.einsum('tme,tpe->tmp', imag_part, xb_imag)
            pred_imag = jnp.einsum('tme,tpe->tmp', imag_part, xb_real) + jnp.einsum('tme,tpe->tmp', real_part, xb_imag)
            resid_real = pred_real - target_real
            resid_imag = pred_imag - target_imag
        resid_real = resid_real.astype(jnp.bfloat16).astype(jnp.float32)
        resid_imag = resid_imag.astype(jnp.bfloat16).astype(jnp.float32)
        grad_real = jnp.einsum('tme,tmp->tpe', real_part, resid_real) + jnp.einsum('tme,tmp->tpe', imag_part, resid_imag)
        grad_imag = jnp.einsum('tme,tmp->tpe', real_part, resid_imag) - jnp.einsum('tme,tmp->tpe', imag_part, resid_real)
        step_real = iter_real - STEP_SIZE * grad_real
        step_imag = iter_imag - STEP_SIZE * grad_imag
        energy = (step_real * step_real + step_imag * step_imag).reshape(ROWS, COLS, E)
        group_norm = jnp.sqrt(group_sum(energy, group_ids))
        factor = jnp.maximum(group_norm - SHRINK_LEVEL, 0.0) / jnp.maximum(group_norm, SHRINK_LEVEL)
        factor = factor.reshape(TILES, pixels, E)
        iter_real = step_real * factor
        iter_imag = step_imag * factor
    result = jnp.concatenate([iter_real, iter_imag], axis=2).reshape(ROWS, COLS, 2 * E)
    return result.astype(jnp.bfloat16)
```

```python
import functools
import math

import jax
import jax.numpy as jnp
from jax import lax
from jax.experimental import pallas as pl
from jax.experimental.pallas import tpu as pltpu
from jax.sharding import PartitionSpec as P

ITERS = 3
BAND = 3
STEP_SIZE = 0.0625
SHRINK_LEVEL = 3.0


def dot(a, b, dims=((1,), (0,))):
    return lax.dot_general(a, b, (dims, ((), ())), preferred_element_type=jnp.float32)


def order_kernel(order_ref, stack_ref, sent_ref):
    acqs, parts, rows, tiles, columns = stack_ref.shape
    lines = acqs * parts * tiles
    share = acqs * parts
    target = lax.broadcasted_iota(jnp.int32, (lines, lines), 0)
    source = lax.broadcasted_iota(jnp.int32, (lines, lines), 1)
    block = lax.rem(source, tiles)
    part = lax.rem(lax.div(source, tiles), parts)
    acq = lax.div(source, tiles * parts)
    tile = jnp.zeros((lines, lines), jnp.int32)
    for k in range(tiles):
        tile = jnp.where(block == k, order_ref[k], tile)
    place = tile * share + part * acqs + acq
    pick = jnp.where(target == place, 1.0, 0.0).astype(jnp.bfloat16)
    for row in range(rows):
        lump = stack_ref[:, :, row].reshape(lines, columns)
        sent_ref[:, row * columns : (row + 1) * columns] = dot(pick, lump).astype(sent_ref.dtype)


def order_tiles(measurements, tile_order):
    acqs, parts, tiles, rows, columns = measurements.shape
    stack = measurements.transpose(0, 1, 3, 2, 4)
    chunk = BAND
    return pl.pallas_call(
        order_kernel,
        grid=(rows // chunk,),
        in_specs=[
            pl.BlockSpec(memory_space=pltpu.SMEM),
            pl.BlockSpec((acqs, parts, chunk, tiles, columns), lambda i: (0, 0, i, 0, 0)),
        ],
        out_specs=pl.BlockSpec((acqs * parts * tiles, chunk * columns), lambda i: (0, i)),
        out_shape=jax.ShapeDtypeStruct((acqs * parts * tiles, rows * columns), measurements.dtype),
        name="order_tiles",
    )(tile_order, stack)


def shrink_factor(energy, pick):
    sums = dot(pick, energy.astype(jnp.bfloat16))
    factor = jnp.maximum(1.0 - SHRINK_LEVEL * lax.rsqrt(jnp.maximum(sums, SHRINK_LEVEL**2)), 0.0)
    high = factor.astype(jnp.bfloat16)
    low = (factor - high.astype(jnp.float32)).astype(jnp.bfloat16)
    both = jnp.concatenate([high, low], axis=0)
    return dot(jnp.concatenate([pick, pick], axis=0), both, ((0,), (0,)))


def band_kernel(
    target_ref, run_ref, back_ref, ahead_ref, out_ref,
    target_sc, resid_sc, step_sc, energy_sc, factor_sc, image_sc, sem,
    *, own_rows, tile_width,
):
    band = pl.program_id(0)
    bands = pl.num_programs(0)
    columns = run_ref.shape[2]
    elevations = factor_sc.shape[1]
    groups = -(-(columns // BAND + 2) // 16) * 16
    first = jnp.where(band == 0, 0, 1)
    later = jnp.where(band == bands - 1, 2, 1)
    weight_of = (first,) + (later,) * (BAND - 1)
    span = [slice(q * columns, (q + 1) * columns) for q in range(BAND)]

    def copies(of):
        return [
            (of * BAND + q - 1, pltpu.make_async_copy(
                image_sc.at[q], out_ref.at[jnp.clip(of * BAND + q - 1, 0, own_rows - 1)], sem.at[q]))
            for q in range(BAND)
        ]

    def drain(of):
        for row, copy in copies(of):
            @pl.when(jnp.logical_and(row >= 0, row < own_rows))
            def _(copy=copy):
                copy.wait()

    group = lax.broadcasted_iota(jnp.int32, (groups, columns), 0)
    pick = jnp.where(group == run_ref[0], 1.0, 0.0).astype(jnp.bfloat16)
    target_sc[...] = target_ref[...].astype(jnp.float32).T

    def descend(is_first):
        for at in range(0, elevations, tile_width):
            real = slice(at, at + tile_width)
            imag = slice(elevations + at, elevations + at + tile_width)
            for q in range(BAND):
                if is_first:
                    resid = target_sc[span[q]].astype(jnp.bfloat16)
                else:
                    resid = resid_sc[span[q]]
                step_real = dot(resid, back_ref[weight_of[q], :, real])
                step_imag = dot(resid, back_ref[weight_of[q], :, imag])
                if not is_first:
                    factor = factor_sc[:, real]
                    step_real += step_sc[span[q], real] * factor
                    step_imag += step_sc[span[q], imag] * factor
                step_sc[span[q], real] = step_real
                step_sc[span[q], imag] = step_imag
                energy = step_real * step_real + step_imag * step_imag
                if q > 0:
                    energy += energy_sc[...]
                if q < BAND - 1:
                    energy_sc[...] = energy
            factor_sc[:, real] = shrink_factor(energy, pick)

    def predict():
        for q in range(BAND):
            guess = jnp.zeros((columns, target_sc.shape[1]), jnp.float32)
            for half in range(2):
                part = slice(half * elevations, (half + 1) * elevations)
                rounded = (step_sc[span[q], part] * factor_sc[...]).astype(jnp.bfloat16)
                guess += dot(rounded, ahead_ref[weight_of[q], part])
            resid_sc[span[q]] = (target_sc[span[q]] - guess).astype(jnp.bfloat16)

    descend(True)

    @pl.loop(1, ITERS)
    def _(i):
        predict()
        descend(False)

    @pl.when(band > 0)
    def _():
        drain(band - 1)

    for q, (row, copy) in enumerate(copies(band)):
        for half in range(2):
            part = slice(half * elevations, (half + 1) * elevations)
            image_sc[q, :, part] = (step_sc[span[q], part] * factor_sc[...]).astype(image_sc.dtype)

        @pl.when(jnp.logical_and(row >= 0, row < own_rows))
        def _(copy=copy):
            copy.start()

    @pl.when(band == bands - 1)
    def _():
        drain(band)


def invert(targets, runs, back, ahead, own_rows, columns):
    lines = targets.shape[0]
    bands = runs.shape[0]
    elevations = back.shape[2] // 2
    whole = pl.BlockSpec(memory_space=pltpu.VMEM)
    pixels = BAND * columns
    tile_width = 256
    return pl.pallas_call(
        functools.partial(band_kernel, own_rows=own_rows, tile_width=tile_width),
        grid=(bands,),
        in_specs=[
            pl.BlockSpec((lines, pixels), lambda i: (0, i)),
            pl.BlockSpec((1, 1, columns), lambda i: (i, 0, 0)),
            whole,
            whole,
        ],
        out_specs=pl.BlockSpec(memory_space=pl.ANY),
        out_shape=jax.ShapeDtypeStruct((own_rows, columns, 2 * elevations), jnp.bfloat16),
        scratch_shapes=[
            pltpu.VMEM((pixels, lines), jnp.float32),
            pltpu.VMEM((pixels, lines), jnp.bfloat16),
            pltpu.VMEM((pixels, 2 * elevations), jnp.float32),
            pltpu.VMEM((columns, tile_width), jnp.float32),
            pltpu.VMEM((columns, elevations), jnp.float32),
            pltpu.VMEM((BAND, columns, 2 * elevations), jnp.bfloat16),
            pltpu.SemaphoreType.DMA((BAND,)),
        ],
        compiler_params=pltpu.CompilerParams(vmem_limit_bytes=40 * 1024 * 1024),
        name="invert",
    )(targets, runs, back, ahead)


def shifted(value, step):
    count = lax.axis_size("acq")
    pairs = [(i, i + step) for i in range(count) if 0 <= i + step < count]
    return lax.ppermute(value, "acq", pairs)


def steering_of(phase, acqs):
    acquisitions = phase.shape[1]
    scale = 1.0 / math.sqrt(acquisitions)
    real = (jnp.cos(phase) * scale).astype(jnp.bfloat16)
    imag = (jnp.sin(phase) * scale).astype(jnp.bfloat16)
    count = phase.shape[0]
    upper = jnp.concatenate([real, -imag], axis=2).reshape(count, -1, 1, acqs, 2 * phase.shape[2])
    lower = jnp.concatenate([imag, real], axis=2).reshape(count, -1, 1, acqs, 2 * phase.shape[2])
    return jnp.concatenate([upper, lower], axis=2).reshape(count, 2 * acquisitions, 2 * phase.shape[2])


def on_device(measurements, tile_order, steer_phase, group_ids):
    acqs = measurements.shape[0]
    rows, columns = group_ids.shape
    assert rows % BAND == 0
    sent = order_tiles(measurements, tile_order)
    targets = lax.all_to_all(sent, "acq", 0, 0, tiled=True)
    phase = jnp.concatenate([shifted(steer_phase, 1), steer_phase, shifted(steer_phase, -1)], axis=0)
    back = steering_of(phase, acqs)
    ahead = back.transpose(0, 2, 1)
    label_rows = [0] + [BAND * b - 1 for b in range(1, rows // BAND + 1)]
    starts = jnp.stack([group_ids[r] for r in label_rows]) % columns
    runs = ((starts + BAND - 1) // BAND)[:, None, :]
    edge = columns * (BAND - 1)
    extended = jnp.concatenate(
        [shifted(targets[:, -columns:], 1), targets, shifted(targets[:, :edge], -1)], axis=1
    )
    return invert(extended, runs, back * STEP_SIZE, ahead, rows, columns)


def solution(mesh):
    placed = (
        P(("groups", "acq"), None, None, None, None),
        P("groups"),
        P(("groups", "acq"), None, None),
        P(("groups", "acq"), None),
    )
    return jax.shard_map(
        on_device,
        mesh=mesh,
        in_specs=placed,
        out_specs=P(("groups", "acq"), None, None),
        check_vma=False,
    )
```

```python
import functools
import math

import jax
import jax.numpy as jnp
from jax import lax
from jax.experimental import pallas as pl
from jax.experimental.pallas import tpu as pltpu
from jax.sharding import PartitionSpec as P


ITERS = 3
BAND = 3
STEP_SIZE = 0.0625
SHRINK_LEVEL = 3.0


def dot(a, b, dims=((1,), (0,))):
    return lax.dot_general(a, b, (dims, ((), ())), preferred_element_type=jnp.float32)


def order_kernel(order_ref, *refs, spans):
    stack_ref, sent_refs = refs[0], refs[1:]
    acqs, parts, _, tiles, columns = stack_ref.shape
    lines = acqs * parts * tiles
    share = acqs * parts
    target = lax.broadcasted_iota(jnp.int32, (lines, 1), 0)
    source = lax.broadcasted_iota(jnp.int32, (1, lines), 1)
    block = lax.rem(source, tiles)
    part = lax.rem(lax.div(source, tiles), parts)
    acq = lax.div(source, tiles * parts)
    tile = jnp.zeros((1, lines), jnp.int32)
    for k in range(tiles):
        tile = jnp.where(block == k, order_ref[k], tile)
    place = tile * share + part * acqs + acq
    pick = jnp.where(target == place, 1.0, 0.0).astype(jnp.bfloat16)
    for sent_ref, span in zip(sent_refs, spans):
        for q, row in enumerate(span):
            lump = stack_ref[:, :, row].reshape(lines, columns)
            sent_ref[:, q * columns : (q + 1) * columns] = dot(pick, lump).astype(sent_ref.dtype)


def order_tiles(measurements, tile_order, spans):
    acqs, parts, tiles, _, columns = measurements.shape
    stack = measurements.transpose(0, 1, 3, 2, 4)
    lines = acqs * parts * tiles
    whole = pl.BlockSpec(memory_space=pltpu.VMEM)
    return pl.pallas_call(
        functools.partial(order_kernel, spans=spans),
        in_specs=[pl.BlockSpec(memory_space=pltpu.SMEM), whole],
        out_specs=[whole] * len(spans),
        out_shape=[
            jax.ShapeDtypeStruct((lines, len(span) * columns), measurements.dtype) for span in spans
        ],
        name="order_tiles",
    )(tile_order, stack)


def shrink_factor(energy, pick):
    sums = dot(pick, energy.astype(jnp.bfloat16))
    factor = jnp.maximum(1.0 - SHRINK_LEVEL * lax.rsqrt(jnp.maximum(sums, SHRINK_LEVEL**2)), 0.0)
    high = factor.astype(jnp.bfloat16)
    low = (factor - high.astype(jnp.float32)).astype(jnp.bfloat16)
    both = jnp.concatenate([high, low], axis=0)
    return dot(jnp.concatenate([pick, pick], axis=0), both, ((0,), (0,)))


def band_kernel(
    target_ref, run_ref, back_ref, ahead_ref, *refs, stride, base, tile_width,
):
    out_ref, target_sc, resid_sc, state_sc, energy_sc, factor_sc, guess_sc, image_sc, sem = refs[-9:]
    own_rows = out_ref.shape[0]
    last_band = own_rows // BAND
    step = pl.program_id(0)
    steps = pl.num_programs(0)
    band = step * stride + base
    columns = run_ref.shape[2]
    elevations = factor_sc.shape[1]
    groups = pick_height(columns)
    weight_of = (1,) * BAND if stride != last_band else (step,) + (step + 1,) * (BAND - 1)
    span = [slice(q * columns, (q + 1) * columns) for q in range(BAND)]
    tiles = [
        (slice(at, at + tile_width), slice(elevations + at, elevations + at + tile_width))
        for at in range(0, elevations, tile_width)
    ]

    def copies(of):
        return [
            (of * BAND + q - 1, pltpu.make_async_copy(
                image_sc.at[q], out_ref.at[jnp.clip(of * BAND + q - 1, 0, own_rows - 1)], sem.at[q]))
            for q in range(BAND)
        ]

    def drain(of):
        for row, copy in copies(of):
            @pl.when(jnp.logical_and(row >= 0, row < own_rows))
            def _(copy=copy):
                copy.wait()

    group = lax.broadcasted_iota(jnp.int32, (groups, columns), 0)
    pick = jnp.where(group == run_ref[0], 1.0, 0.0).astype(jnp.bfloat16)
    target_sc[...] = target_ref[...].T

    @pl.when(step > 0)
    def _():
        drain(band - stride)

    for i in range(ITERS):
        for t, (real, imag) in enumerate(tiles):
            for q in range(BAND):
                resid = target_sc[span[q]] if i == 0 else resid_sc[span[q]]
                step_real = dot(resid, back_ref[weight_of[q], :, real])
                step_imag = dot(resid, back_ref[weight_of[q], :, imag])
                if i > 0:
                    step_real += state_sc[span[q], real]
                    step_imag += state_sc[span[q], imag]
                state_sc[span[q], real] = step_real
                state_sc[span[q], imag] = step_imag
                energy = step_real * step_real + step_imag * step_imag
                if q > 0:
                    energy += energy_sc[t]
                if q < BAND - 1:
                    energy_sc[t] = energy
            factor_sc[:, real] = shrink_factor(energy, pick)
            for q in range(BAND):
                factor = factor_sc[:, real]
                new_real = state_sc[span[q], real] * factor
                new_imag = state_sc[span[q], imag] * factor
                if i == ITERS - 1:
                    image_sc[q, :, real] = new_real.astype(image_sc.dtype)
                    image_sc[q, :, imag] = new_imag.astype(image_sc.dtype)
                    continue
                state_sc[span[q], real] = new_real
                state_sc[span[q], imag] = new_imag
                rounded = jnp.concatenate([new_real, new_imag], axis=1).astype(jnp.bfloat16)
                weights = jnp.concatenate(
                    [ahead_ref[weight_of[q], real], ahead_ref[weight_of[q], imag]], axis=0
                )
                guess = dot(rounded, weights)
                if t > 0:
                    guess += guess_sc[span[q]]
                if t < len(tiles) - 1:
                    guess_sc[span[q]] = guess
                else:
                    resid_sc[span[q]] = (target_sc[span[q]].astype(jnp.float32) - guess).astype(
                        jnp.bfloat16
                    )

    for row, copy in copies(band):
        @pl.when(jnp.logical_and(row >= 0, row < own_rows))
        def _(copy=copy):
            copy.start()

    @pl.when(step == steps - 1)
    def _():
        drain(band)


def pick_height(columns):
    return -(-(columns // BAND + 2) // 16) * 16


def invert(targets, runs, back, ahead, out, out_shape, base, stride):
    lines = targets.shape[0]
    steps = runs.shape[0]
    columns = runs.shape[2]
    elevations = back.shape[2] // 2
    whole = pl.BlockSpec(memory_space=pltpu.VMEM)
    far = pl.BlockSpec(memory_space=pl.ANY)
    pixels = BAND * columns
    tile_width = 256
    held = () if out is None else (out,)
    return pl.pallas_call(
        functools.partial(band_kernel, base=base, stride=stride, tile_width=tile_width),
        grid=(steps,),
        in_specs=[
            pl.BlockSpec((lines, pixels), lambda i: (0, i)),
            pl.BlockSpec((1, 1, columns), lambda i: (i, 0, 0)),
            whole,
            whole,
        ]
        + [far] * len(held),
        out_specs=far,
        out_shape=jax.ShapeDtypeStruct(out_shape, jnp.bfloat16),
        input_output_aliases={4: 0} if held else {},
        scratch_shapes=[
            pltpu.VMEM((pixels, lines), jnp.bfloat16),
            pltpu.VMEM((pixels, lines), jnp.bfloat16),
            pltpu.VMEM((pixels, 2 * elevations), jnp.float32),
            pltpu.VMEM((elevations // tile_width, columns, tile_width), jnp.float32),
            pltpu.VMEM((columns, elevations), jnp.float32),
            pltpu.VMEM((pixels, lines), jnp.float32),
            pltpu.VMEM((BAND, columns, 2 * elevations), jnp.bfloat16),
            pltpu.SemaphoreType.DMA((BAND,)),
        ],
        compiler_params=pltpu.CompilerParams(vmem_limit_bytes=40 * 1024 * 1024),
        name="invert",
    )(targets, runs, back, ahead, *held)


def shifted(value, step):
    count = lax.axis_size("acq")
    pairs = [(i, i + step) for i in range(count) if 0 <= i + step < count]
    return lax.ppermute(value, "acq", pairs)


def steering_of(phase, acqs):
    acquisitions = phase.shape[1]
    scale = 1.0 / math.sqrt(acquisitions)
    real = (jnp.cos(phase) * scale).astype(jnp.bfloat16)
    imag = (jnp.sin(phase) * scale).astype(jnp.bfloat16)
    count = phase.shape[0]
    upper = jnp.concatenate([real, -imag], axis=2).reshape(count, -1, 1, acqs, 2 * phase.shape[2])
    lower = jnp.concatenate([imag, real], axis=2).reshape(count, -1, 1, acqs, 2 * phase.shape[2])
    return jnp.concatenate([upper, lower], axis=2).reshape(count, 2 * acquisitions, 2 * phase.shape[2])


def program(measurements, tile_order, steer_phase, group_ids):
    acqs = measurements.shape[0]
    rows, columns = group_ids.shape
    elevations = steer_phase.shape[2]
    assert rows % BAND == 0
    bands = rows // BAND
    edge = [rows - 1] + list(range(BAND - 1))
    inner = [list(range(BAND * b - 1, BAND * b + 2)) for b in range(1, bands)]
    early = 1
    spans = [edge + sum(inner[:early], []), sum(inner[early:], [])]
    sent = order_tiles(measurements, tile_order, spans)
    head = lax.all_to_all(sent[0], "acq", 0, 0, tiled=True)
    tail = lax.all_to_all(sent[1], "acq", 0, 0, tiled=True)
    phase = jnp.concatenate(
        [shifted(steer_phase, 1), steer_phase, shifted(steer_phase, -1)], axis=0
    )
    back = steering_of(phase, acqs)
    ahead = back.transpose(0, 2, 1)
    back = back * STEP_SIZE
    runs = ((group_ids % columns + BAND - 1) // BAND)[:, None, :]
    runs_of = [runs[max(BAND * b - 1, 0)] for b in range(bands + 1)]
    width = BAND * columns
    above, below = head[:, :columns], head[:, columns:width]
    targets = jnp.concatenate([shifted(above, 1), below, above, shifted(below, -1)], axis=1)
    shape = (rows, columns, 2 * elevations)
    out = invert(targets, jnp.stack([runs_of[0], runs_of[-1]]), back, ahead, None, shape, 0, bands)
    mine = jnp.stack(runs_of[1 : 1 + early])
    out = invert(head[:, width:], mine, back, ahead, out, shape, 1, 1)
    mine = jnp.stack(runs_of[1 + early : bands])
    out = invert(tail, mine, back, ahead, out, shape, 1 + early, 1)
    return out


def solution(mesh):
    placed = (
        P(("groups", "acq"), None, None, None, None),
        P("groups"),
        P(("groups", "acq"), None, None),
        P(("groups", "acq"), None),
    )
    return jax.shard_map(
        program,
        mesh=mesh,
        in_specs=placed,
        out_specs=P(("groups", "acq"), None, None),
        check_vma=False,
    )
```

```python
import functools
import math

import jax
import jax.numpy as jnp
from jax import lax
from jax.experimental import pallas as pl
from jax.experimental.pallas import tpu as pltpu
from jax.sharding import PartitionSpec as P


ITERS = 3
BAND = 3
STEP_SIZE = 0.0625
SHRINK_LEVEL = 3.0


def dot(a, b, dims=((1,), (0,))):
    return lax.dot_general(a, b, (dims, ((), ())), preferred_element_type=jnp.float32)


def order_kernel(order_ref, *refs, spans):
    stack_ref, sent_refs = refs[0], refs[1:]
    acqs, parts, _, tiles, columns = stack_ref.shape
    lines = acqs * parts * tiles
    share = acqs * parts
    target = lax.broadcasted_iota(jnp.int32, (lines, 1), 0)
    source = lax.broadcasted_iota(jnp.int32, (1, lines), 1)
    block = lax.rem(source, tiles)
    part = lax.rem(lax.div(source, tiles), parts)
    acq = lax.div(source, tiles * parts)
    tile = jnp.zeros((1, lines), jnp.int32)
    for k in range(tiles):
        tile = jnp.where(block == k, order_ref[k], tile)
    place = tile * share + part * acqs + acq
    pick = jnp.where(target == place, 1.0, 0.0).astype(jnp.bfloat16)
    for sent_ref, span in zip(sent_refs, spans):
        for q, row in enumerate(span):
            lump = stack_ref[:, :, row].reshape(lines, columns)
            sent_ref[:, q * columns : (q + 1) * columns] = dot(pick, lump).astype(sent_ref.dtype)


def order_tiles(measurements, tile_order, spans):
    acqs, parts, tiles, _, columns = measurements.shape
    stack = measurements.transpose(0, 1, 3, 2, 4)
    lines = acqs * parts * tiles
    whole = pl.BlockSpec(memory_space=pltpu.VMEM)
    return pl.pallas_call(
        functools.partial(order_kernel, spans=spans),
        in_specs=[pl.BlockSpec(memory_space=pltpu.SMEM), whole],
        out_specs=[whole] * len(spans),
        out_shape=[
            jax.ShapeDtypeStruct((lines, len(span) * columns), measurements.dtype) for span in spans
        ],
        name="order_tiles",
    )(tile_order, stack)


def shrink_factor(energy, pick):
    sums = dot(pick, energy.astype(jnp.bfloat16))
    factor = jnp.maximum(1.0 - SHRINK_LEVEL * lax.rsqrt(jnp.maximum(sums, SHRINK_LEVEL**2)), 0.0)
    high = factor.astype(jnp.bfloat16)
    low = (factor - high.astype(jnp.float32)).astype(jnp.bfloat16)
    both = jnp.concatenate([high, low], axis=0)
    return dot(jnp.concatenate([pick, pick], axis=0), both, ((0,), (0,)))


def band_kernel(
    target_ref, run_ref, back_ref, ahead_ref, *refs, stride, base, tile_width,
):
    out_ref, target_sc, resid_sc, step_sc, energy_sc, factor_sc, image_sc, sem = refs[-8:]
    own_rows = out_ref.shape[0]
    last_band = own_rows // BAND
    step = pl.program_id(0)
    steps = pl.num_programs(0)
    band = step * stride + base
    columns = run_ref.shape[2]
    elevations = factor_sc.shape[1]
    groups = -(-(columns // BAND + 2) // 16) * 16
    weight_of = (1,) * BAND if stride != last_band else (step,) + (step + 1,) * (BAND - 1)
    span = [slice(q * columns, (q + 1) * columns) for q in range(BAND)]

    def copies(of):
        return [
            (of * BAND + q - 1, pltpu.make_async_copy(
                image_sc.at[q], out_ref.at[jnp.clip(of * BAND + q - 1, 0, own_rows - 1)], sem.at[q]))
            for q in range(BAND)
        ]

    def drain(of):
        for row, copy in copies(of):
            @pl.when(jnp.logical_and(row >= 0, row < own_rows))
            def _(copy=copy):
                copy.wait()

    group = lax.broadcasted_iota(jnp.int32, (groups, columns), 0)
    pick = jnp.where(group == run_ref[0], 1.0, 0.0).astype(jnp.bfloat16)
    target_sc[...] = target_ref[...].astype(jnp.float32).T

    def descend(is_first):
        for at in range(0, elevations, tile_width):
            real = slice(at, at + tile_width)
            imag = slice(elevations + at, elevations + at + tile_width)
            for q in range(BAND):
                if is_first:
                    resid = target_sc[span[q]].astype(jnp.bfloat16)
                else:
                    resid = resid_sc[span[q]]
                step_real = dot(resid, back_ref[weight_of[q], :, real])
                step_imag = dot(resid, back_ref[weight_of[q], :, imag])
                if not is_first:
                    factor = factor_sc[:, real]
                    step_real += step_sc[span[q], real] * factor
                    step_imag += step_sc[span[q], imag] * factor
                step_sc[span[q], real] = step_real
                step_sc[span[q], imag] = step_imag
                energy = step_real * step_real + step_imag * step_imag
                if q > 0:
                    energy += energy_sc[...]
                if q < BAND - 1:
                    energy_sc[...] = energy
            factor_sc[:, real] = shrink_factor(energy, pick)

    def predict():
        for q in range(BAND):
            guess = jnp.zeros((columns, target_sc.shape[1]), jnp.float32)
            for half in range(2):
                part = slice(half * elevations, (half + 1) * elevations)
                rounded = (step_sc[span[q], part] * factor_sc[...]).astype(jnp.bfloat16)
                guess += dot(rounded, ahead_ref[weight_of[q], part])
            resid_sc[span[q]] = (target_sc[span[q]] - guess).astype(jnp.bfloat16)

    descend(True)

    @pl.loop(1, ITERS)
    def _(i):
        predict()
        descend(False)

    @pl.when(step > 0)
    def _():
        drain(band - stride)

    for q, (row, copy) in enumerate(copies(band)):
        for half in range(2):
            part = slice(half * elevations, (half + 1) * elevations)
            image_sc[q, :, part] = (step_sc[span[q], part] * factor_sc[...]).astype(image_sc.dtype)

        @pl.when(jnp.logical_and(row >= 0, row < own_rows))
        def _(copy=copy):
            copy.start()

    @pl.when(step == steps - 1)
    def _():
        drain(band)


def invert(targets, runs, back, ahead, out, out_shape, base, stride):
    lines = targets.shape[0]
    steps = runs.shape[0]
    columns = runs.shape[2]
    elevations = back.shape[2] // 2
    whole = pl.BlockSpec(memory_space=pltpu.VMEM)
    far = pl.BlockSpec(memory_space=pl.ANY)
    pixels = BAND * columns
    tile_width = 256
    held = () if out is None else (out,)
    return pl.pallas_call(
        functools.partial(band_kernel, base=base, stride=stride, tile_width=tile_width),
        grid=(steps,),
        in_specs=[
            pl.BlockSpec((lines, pixels), lambda i: (0, i)),
            pl.BlockSpec((1, 1, columns), lambda i: (i, 0, 0)),
            whole,
            whole,
        ]
        + [far] * len(held),
        out_specs=far,
        out_shape=jax.ShapeDtypeStruct(out_shape, jnp.bfloat16),
        input_output_aliases={4: 0} if held else {},
        scratch_shapes=[
            pltpu.VMEM((pixels, lines), jnp.float32),
            pltpu.VMEM((pixels, lines), jnp.bfloat16),
            pltpu.VMEM((pixels, 2 * elevations), jnp.float32),
            pltpu.VMEM((columns, tile_width), jnp.float32),
            pltpu.VMEM((columns, elevations), jnp.float32),
            pltpu.VMEM((BAND, columns, 2 * elevations), jnp.bfloat16),
            pltpu.SemaphoreType.DMA((BAND,)),
        ],
        compiler_params=pltpu.CompilerParams(vmem_limit_bytes=40 * 1024 * 1024),
        name="invert",
    )(targets, runs, back, ahead, *held)


def shifted(value, step):
    count = lax.axis_size("acq")
    pairs = [(i, i + step) for i in range(count) if 0 <= i + step < count]
    return lax.ppermute(value, "acq", pairs)


def steering_of(phase):
    scale = 1.0 / math.sqrt(phase.shape[1])
    real = (jnp.cos(phase) * scale).astype(jnp.bfloat16)
    imag = (jnp.sin(phase) * scale).astype(jnp.bfloat16)
    return jnp.concatenate([real, imag], axis=1)


def planes_of(steering, acqs):
    count, lines, elevations = steering.shape
    real, imag = steering[:, : lines // 2], steering[:, lines // 2 :]
    upper = jnp.concatenate([real, -imag], axis=2).reshape(count, -1, 1, acqs, 2 * elevations)
    lower = jnp.concatenate([imag, real], axis=2).reshape(count, -1, 1, acqs, 2 * elevations)
    return jnp.concatenate([upper, lower], axis=2).reshape(count, lines, 2 * elevations)


def program(measurements, tile_order, steer_phase, group_ids):
    acqs = measurements.shape[0]
    rows, columns = group_ids.shape
    elevations = steer_phase.shape[2]
    assert rows % BAND == 0
    bands = rows // BAND
    edge = [rows - 1] + list(range(BAND - 1))
    inner = [list(range(BAND * b - 1, BAND * b + 2)) for b in range(1, bands)]
    early = 1
    spans = [edge + sum(inner[:early], []), sum(inner[early:], [])]
    sent = order_tiles(measurements, tile_order, spans)
    head = lax.all_to_all(sent[0], "acq", 0, 0, tiled=True)
    tail = lax.all_to_all(sent[1], "acq", 0, 0, tiled=True)
    mine = steering_of(steer_phase)
    steering = jnp.concatenate([shifted(mine, 1), mine, shifted(mine, -1)], axis=0)
    back = planes_of(steering, acqs)
    ahead = back.transpose(0, 2, 1)
    back = back * STEP_SIZE
    runs = ((group_ids % columns + BAND - 1) // BAND)[:, None, :]
    runs_of = [runs[max(BAND * b - 1, 0)] for b in range(bands + 1)]
    width = BAND * columns
    above, below = head[:, :columns], head[:, columns:width]
    targets = jnp.concatenate([shifted(above, 1), below, above, shifted(below, -1)], axis=1)
    shape = (rows, columns, 2 * elevations)
    out = invert(targets, jnp.stack([runs_of[0], runs_of[-1]]), back, ahead, None, shape, 0, bands)
    mine = jnp.stack(runs_of[1 : 1 + early])
    out = invert(head[:, width:], mine, back, ahead, out, shape, 1, 1)
    mine = jnp.stack(runs_of[1 + early : bands])
    out = invert(tail, mine, back, ahead, out, shape, 1 + early, 1)
    return out


def solution(mesh):
    placed = (
        P(("groups", "acq"), None, None, None, None),
        P("groups"),
        P(("groups", "acq"), None, None),
        P(("groups", "acq"), None),
    )
    return jax.shard_map(
        program,
        mesh=mesh,
        in_specs=placed,
        out_specs=P(("groups", "acq"), None, None),
        check_vma=False,
    )
```

```python
import functools
import math

import jax
import jax.numpy as jnp
from jax import lax
from jax.experimental import pallas as pl
from jax.experimental.pallas import tpu as pltpu
from jax.sharding import PartitionSpec as P


ITERS = 3
BAND = 3
STEP_SIZE = 0.0625
SHRINK_LEVEL = 3.0


def dot(a, b, dims=((1,), (0,))):
    return lax.dot_general(a, b, (dims, ((), ())), preferred_element_type=jnp.float32)


def order_kernel(order_ref, *refs, spans, ahead_rows):
    stack_ref, sent_refs = refs[0], refs[1:]
    acqs, parts, _, tiles, columns = stack_ref.shape
    lines = acqs * parts * tiles
    share = acqs * parts
    target = lax.broadcasted_iota(jnp.int32, (lines, 1), 0)
    source = lax.broadcasted_iota(jnp.int32, (1, lines), 1)
    block = lax.rem(source, tiles)
    part = lax.rem(lax.div(source, tiles), parts)
    acq = lax.div(source, tiles * parts)
    tile = jnp.zeros((1, lines), jnp.int32)
    for k in range(tiles):
        tile = jnp.where(block == k, order_ref[k], tile)
    after = jnp.where(tile == tiles - 1, 0, tile + 1)
    inner = part * acqs + acq
    pick = jnp.where(target == tile * share + inner, 1.0, 0.0).astype(jnp.bfloat16)
    pick_after = jnp.where(target == after * share + inner, 1.0, 0.0).astype(jnp.bfloat16)
    for sent_ref, span in zip(sent_refs, spans):
        for q, row in enumerate(span):
            lump = stack_ref[:, :, row].reshape(lines, columns)
            chosen = pick_after if row in ahead_rows else pick
            sent_ref[:, q * columns : (q + 1) * columns] = dot(chosen, lump).astype(sent_ref.dtype)


def order_tiles(measurements, tile_order, spans, ahead_rows):
    acqs, parts, tiles, _, columns = measurements.shape
    stack = measurements.transpose(0, 1, 3, 2, 4)
    lines = acqs * parts * tiles
    whole = pl.BlockSpec(memory_space=pltpu.VMEM)
    return pl.pallas_call(
        functools.partial(order_kernel, spans=spans, ahead_rows=ahead_rows),
        in_specs=[pl.BlockSpec(memory_space=pltpu.SMEM), whole],
        out_specs=[whole] * len(spans),
        out_shape=[
            jax.ShapeDtypeStruct((lines, len(span) * columns), measurements.dtype) for span in spans
        ],
        name="order_tiles",
    )(tile_order, stack)


def run_sums(energy, pick):
    return dot(pick, energy.astype(jnp.bfloat16))


def shrink_factor(sums, pick):
    factor = jnp.maximum(1.0 - SHRINK_LEVEL * lax.rsqrt(jnp.maximum(sums, SHRINK_LEVEL**2)), 0.0)
    high = factor.astype(jnp.bfloat16)
    low = (factor - high.astype(jnp.float32)).astype(jnp.bfloat16)
    both = jnp.concatenate([high, low], axis=0)
    return dot(jnp.concatenate([pick, pick], axis=0), both, ((0,), (0,)))


def band_kernel(joined_ref, target_ref, run_ref, back_ref, ahead_ref, *refs, edge, base, held, late):
    refs = list(refs)
    if held:
        refs.pop(0)
    late_ref = refs.pop(0) if late else None
    out_ref = refs.pop(0)
    above_ref = refs.pop(0) if edge else None
    target_sc, resid_sc, step_sc, energy_sc, factor_sc, image_sc, sem = refs
    step = pl.program_id(0)
    steps = pl.num_programs(0)
    columns = run_ref.shape[2]
    elevations = factor_sc.shape[2]
    tile_width = energy_sc.shape[2]
    groups = -(-(columns // BAND + 2) // 16) * 16
    weight_of = (0 if edge else 1,) + (1,) * (BAND - 1)
    set_of = weight_of
    span = [slice(q * columns, (q + 1) * columns) for q in range(BAND)]

    def copies(of):
        first = BAND * (base + of) - 1
        targets = [above_ref if edge and q == 0 else out_ref.at[first + q] for q in range(BAND)]
        pairs = [pltpu.make_async_copy(image_sc.at[q], targets[q], sem.at[q]) for q in range(BAND)]
        if late:
            pairs.append(pltpu.make_async_copy(late_ref, out_ref.at[out_ref.shape[0] - 1], sem.at[BAND]))
        return pairs

    group = lax.broadcasted_iota(jnp.int32, (groups, columns), 0)
    picks = [
        jnp.where(group == run_ref[0, n : n + 1], 1.0, 0.0).astype(jnp.bfloat16)
        for n in range(run_ref.shape[1])
    ]
    target_sc[...] = target_ref[...].astype(jnp.float32).T

    def descend(is_first):
        for at in range(0, elevations, tile_width):
            real = slice(at, at + tile_width)
            imag = slice(elevations + at, elevations + at + tile_width)
            for q in range(BAND):
                if is_first:
                    resid = target_sc[span[q]].astype(jnp.bfloat16)
                else:
                    resid = resid_sc[span[q]]
                step_real = dot(resid, back_ref[weight_of[q], :, real])
                step_imag = dot(resid, back_ref[weight_of[q], :, imag])
                if not is_first:
                    factor = factor_sc[set_of[q], :, real]
                    step_real += step_sc[span[q], real] * factor
                    step_imag += step_sc[span[q], imag] * factor
                step_sc[span[q], real] = step_real
                step_sc[span[q], imag] = step_imag
                energy = step_real * step_real + step_imag * step_imag
                if q > 0 and set_of[q] == set_of[q - 1]:
                    energy += energy_sc[set_of[q]]
                if q < BAND - 1:
                    energy_sc[set_of[q]] = energy
            sums = run_sums(energy, picks[-1])
            if edge:
                apart = run_sums(energy_sc[0], picks[0])
                joined = joined_ref[0] > 0
                factor_sc[0, :, real] = shrink_factor(
                    jnp.where(joined, apart + sums, apart), picks[0]
                )
                sums = jnp.where(joined, apart + sums, sums)
            factor_sc[1, :, real] = shrink_factor(sums, picks[-1])

    def predict():
        for q in range(BAND):
            guess = jnp.zeros((columns, target_sc.shape[1]), jnp.float32)
            for half in range(2):
                part = slice(half * elevations, (half + 1) * elevations)
                rounded = (step_sc[span[q], part] * factor_sc[set_of[q]]).astype(jnp.bfloat16)
                guess += dot(rounded, ahead_ref[weight_of[q], part])
            resid_sc[span[q]] = (target_sc[span[q]] - guess).astype(jnp.bfloat16)

    descend(True)

    @pl.loop(1, ITERS)
    def _(i):
        predict()
        descend(False)

    @pl.when(step > 0)
    def _():
        for copy in copies(step - 1)[:BAND]:
            copy.wait()

    for q in range(BAND):
        for half in range(2):
            part = slice(half * elevations, (half + 1) * elevations)
            image_sc[q, :, part] = (step_sc[span[q], part] * factor_sc[set_of[q]]).astype(
                image_sc.dtype
            )
        copies(step)[q].start()

    @pl.when(step == steps - 1)
    def _():
        if late:
            copies(step)[BAND].start()
        for copy in copies(step):
            copy.wait()


def invert(joined, targets, runs, back, ahead, out_shape, *, offset, base, edge=False, out=None, late=None):
    lines = targets.shape[0]
    steps, kinds, columns = runs.shape
    elevations = back.shape[2] // 2
    whole = pl.BlockSpec(memory_space=pltpu.VMEM)
    far = pl.BlockSpec(memory_space=pl.ANY)
    pixels = BAND * columns
    tile_width = 256
    shape = jax.ShapeDtypeStruct(out_shape, jnp.bfloat16)
    above = jax.ShapeDtypeStruct(out_shape[1:], jnp.bfloat16)
    extra = ([] if out is None else [out]) + ([] if late is None else [late])
    extra_specs = ([] if out is None else [far]) + ([] if late is None else [whole])
    return pl.pallas_call(
        functools.partial(
            band_kernel, edge=edge, base=base, held=out is not None, late=late is not None
        ),
        grid=(steps,),
        in_specs=[
            pl.BlockSpec(memory_space=pltpu.SMEM),
            pl.BlockSpec((lines, pixels), lambda i: (0, i + offset)),
            pl.BlockSpec((1, kinds, columns), lambda i: (i, 0, 0)),
            whole,
            whole,
        ]
        + extra_specs,
        out_specs=[far, far] if edge else far,
        out_shape=[shape, above] if edge else shape,
        input_output_aliases={} if out is None else {5: 0},
        scratch_shapes=[
            pltpu.VMEM((pixels, lines), jnp.float32),
            pltpu.VMEM((pixels, lines), jnp.bfloat16),
            pltpu.VMEM((pixels, 2 * elevations), jnp.float32),
            pltpu.VMEM((2, columns, tile_width), jnp.float32),
            pltpu.VMEM((2, columns, elevations), jnp.float32),
            pltpu.VMEM((BAND, columns, 2 * elevations), jnp.bfloat16),
            pltpu.SemaphoreType.DMA((BAND + 1,)),
        ],
        compiler_params=pltpu.CompilerParams(vmem_limit_bytes=40 * 1024 * 1024),
        name="invert_edge" if edge else "invert",
    )(joined, targets, runs, back, ahead, *extra)


def turned(value, step):
    count = lax.axis_size("acq")
    return lax.ppermute(value, "acq", [(i, (i + step) % count) for i in range(count)])


def steering_of(phase):
    scale = 1.0 / math.sqrt(phase.shape[1])
    real = (jnp.cos(phase) * scale).astype(jnp.bfloat16)
    imag = (jnp.sin(phase) * scale).astype(jnp.bfloat16)
    return jnp.concatenate([real, imag], axis=1)


def planes_of(steering, acqs):
    count, lines, elevations = steering.shape
    real, imag = steering[:, : lines // 2], steering[:, lines // 2 :]
    upper = jnp.concatenate([real, -imag], axis=2).reshape(count, -1, 1, acqs, 2 * elevations)
    lower = jnp.concatenate([imag, real], axis=2).reshape(count, -1, 1, acqs, 2 * elevations)
    return jnp.concatenate([upper, lower], axis=2).reshape(count, lines, 2 * elevations)


def program(measurements, tile_order, steer_phase, group_ids):
    acqs = measurements.shape[0]
    rows, columns = group_ids.shape
    elevations = steer_phase.shape[2]
    assert rows % BAND == 0
    bands = rows // BAND
    edge = [rows - 1] + list(range(BAND - 1))
    inner = [list(range(BAND * b - 1, BAND * b + 2)) for b in range(1, bands)]
    early = 1
    spans = [edge + sum(inner[:early], []), sum(inner[early:], [])]
    sent = order_tiles(measurements, tile_order, spans, (rows - 1,))
    head = lax.all_to_all(sent[0], "acq", 0, 0, tiled=True)
    tail = lax.all_to_all(sent[1], "acq", 0, 0, tiled=True)
    mine = steering_of(steer_phase)
    steering = jnp.concatenate([turned(mine, 1), mine], axis=0)
    back = planes_of(steering, acqs)
    ahead = back.transpose(0, 2, 1)
    back = back * STEP_SIZE
    runs = (group_ids % columns + BAND - 1) // BAND
    first = lax.axis_index("acq") == 0
    column = jnp.arange(columns, dtype=jnp.int32)
    turn = (columns - 1) % BAND
    last_starts = jnp.maximum(0, BAND * ((column - turn + BAND) // BAND) - BAND + turn)
    last_runs = (last_starts + BAND - 1) // BAND
    edge_runs = jnp.stack([jnp.where(first, last_runs, runs[0]), runs[0]])[None]
    inner_runs = runs[BAND - 1 : rows - 1 : BAND][:, None]
    joined = jnp.where(first, 0, 1).reshape(1)
    shape = (rows, columns, 2 * elevations)
    out, above = invert(joined, head, edge_runs, back, ahead, shape, offset=0, base=0, edge=True)
    late = turned(above, -1)
    out = invert(joined, head, inner_runs[:early], back, ahead, shape, offset=1, base=1, out=out)
    return invert(
        joined, tail, inner_runs[early:], back, ahead, shape,
        offset=0, base=1 + early, out=out, late=late,
    )


def solution(mesh):
    placed = (
        P(("groups", "acq"), None, None, None, None),
        P("groups"),
        P(("groups", "acq"), None, None),
        P(("groups", "acq"), None),
    )
    return jax.shard_map(
        program,
        mesh=mesh,
        in_specs=placed,
        out_specs=P(("groups", "acq"), None, None),
        check_vma=False,
    )
```

```python
import functools
import math

import jax
import jax.numpy as jnp
from jax import lax
from jax.experimental import pallas as pl
from jax.experimental.pallas import tpu as pltpu
from jax.sharding import PartitionSpec as P


ITERS = 3
BAND = 3
STEP_SIZE = 0.0625
SHRINK_LEVEL = 3.0


def dot(a, b, dims=((1,), (0,))):
    return lax.dot_general(a, b, (dims, ((), ())), preferred_element_type=jnp.float32)


def order_kernel(order_ref, *refs, spans, ahead_rows):
    stack_ref, sent_refs = refs[0], refs[1:]
    acqs, parts, _, tiles, columns = stack_ref.shape
    lines = acqs * parts * tiles
    share = acqs * parts
    target = lax.broadcasted_iota(jnp.int32, (lines, 1), 0)
    source = lax.broadcasted_iota(jnp.int32, (1, lines), 1)
    block = lax.rem(source, tiles)
    part = lax.rem(lax.div(source, tiles), parts)
    acq = lax.div(source, tiles * parts)
    tile = jnp.zeros((1, lines), jnp.int32)
    for k in range(tiles):
        tile = jnp.where(block == k, order_ref[k], tile)
    after = jnp.where(tile == tiles - 1, 0, tile + 1)
    inner = part * acqs + acq
    pick = jnp.where(target == tile * share + inner, 1.0, 0.0).astype(jnp.bfloat16)
    pick_after = jnp.where(target == after * share + inner, 1.0, 0.0).astype(jnp.bfloat16)
    for sent_ref, span in zip(sent_refs, spans):
        for q, row in enumerate(span):
            lump = stack_ref[:, :, row].reshape(lines, columns)
            chosen = pick_after if row in ahead_rows else pick
            sent_ref[:, q * columns : (q + 1) * columns] = dot(chosen, lump).astype(sent_ref.dtype)


def order_tiles(measurements, tile_order, spans, ahead_rows):
    acqs, parts, tiles, _, columns = measurements.shape
    stack = measurements.transpose(0, 1, 3, 2, 4)
    lines = acqs * parts * tiles
    whole = pl.BlockSpec(memory_space=pltpu.VMEM)
    return pl.pallas_call(
        functools.partial(order_kernel, spans=spans, ahead_rows=ahead_rows),
        in_specs=[pl.BlockSpec(memory_space=pltpu.SMEM), whole],
        out_specs=[whole] * len(spans),
        out_shape=[
            jax.ShapeDtypeStruct((lines, len(span) * columns), measurements.dtype) for span in spans
        ],
        name="order_tiles",
    )(tile_order, stack)


def run_sums(energy, pick):
    return dot(pick, energy.astype(jnp.bfloat16))


def shrink_factor(sums, pick):
    factor = jnp.maximum(1.0 - SHRINK_LEVEL * lax.rsqrt(jnp.maximum(sums, SHRINK_LEVEL**2)), 0.0)
    high = factor.astype(jnp.bfloat16)
    low = (factor - high.astype(jnp.float32)).astype(jnp.bfloat16)
    both = jnp.concatenate([high, low], axis=0)
    return dot(jnp.concatenate([pick, pick], axis=0), both, ((0,), (0,)))


def band_kernel(joined_ref, target_ref, run_ref, back_ref, ahead_ref, *refs, edge, base, held, late):
    refs = list(refs)
    if held:
        refs.pop(0)
    late_ref = refs.pop(0) if late else None
    out_ref = refs.pop(0)
    above_ref = refs.pop(0) if edge else None
    target_sc, resid_sc, step_sc, energy_sc, factor_sc, image_sc, sem = refs
    step = pl.program_id(0)
    steps = pl.num_programs(0)
    columns = run_ref.shape[2]
    elevations = factor_sc.shape[2]
    tile_width = energy_sc.shape[2]
    groups = -(-(columns // BAND + 2) // 16) * 16
    weight_of = (0 if edge else 1,) + (1,) * (BAND - 1)
    set_of = weight_of
    span = [slice(q * columns, (q + 1) * columns) for q in range(BAND)]

    def copies(of):
        first = BAND * (base + of) - 1
        targets = [above_ref if edge and q == 0 else out_ref.at[first + q] for q in range(BAND)]
        pairs = [pltpu.make_async_copy(image_sc.at[q], targets[q], sem.at[q]) for q in range(BAND)]
        if late:
            pairs.append(pltpu.make_async_copy(late_ref, out_ref.at[out_ref.shape[0] - 1], sem.at[BAND]))
        return pairs

    group = lax.broadcasted_iota(jnp.int32, (groups, columns), 0)
    picks = [
        jnp.where(group == run_ref[0, n : n + 1], 1.0, 0.0).astype(jnp.bfloat16)
        for n in range(run_ref.shape[1])
    ]
    target_sc[...] = target_ref[...].astype(jnp.float32).T

    def descend(is_first):
        for at in range(0, elevations, tile_width):
            real = slice(at, at + tile_width)
            imag = slice(elevations + at, elevations + at + tile_width)
            for q in range(BAND):
                if is_first:
                    resid = target_sc[span[q]].astype(jnp.bfloat16)
                else:
                    resid = resid_sc[span[q]]
                step_real = dot(resid, back_ref[weight_of[q], :, real])
                step_imag = dot(resid, back_ref[weight_of[q], :, imag])
                if not is_first:
                    factor = factor_sc[set_of[q], :, real]
                    step_real += step_sc[span[q], real] * factor
                    step_imag += step_sc[span[q], imag] * factor
                step_sc[span[q], real] = step_real
                step_sc[span[q], imag] = step_imag
                energy = step_real * step_real + step_imag * step_imag
                slot = 2 * (at // tile_width) + set_of[q]
                if q > 0 and set_of[q] == set_of[q - 1]:
                    energy += energy_sc[slot]
                energy_sc[slot] = energy

        for at in range(0, elevations, tile_width):
            real = slice(at, at + tile_width)
            slot = 2 * (at // tile_width)
            sums = run_sums(energy_sc[slot + 1], picks[-1])
            if edge:
                apart = run_sums(energy_sc[slot], picks[0])
                joined = joined_ref[0] > 0
                factor_sc[0, :, real] = shrink_factor(
                    jnp.where(joined, apart + sums, apart), picks[0]
                )
                sums = jnp.where(joined, apart + sums, sums)
            factor_sc[1, :, real] = shrink_factor(sums, picks[-1])

    def predict():
        for q in range(BAND):
            guess = jnp.zeros((columns, target_sc.shape[1]), jnp.float32)
            for half in range(2):
                part = slice(half * elevations, (half + 1) * elevations)
                rounded = (step_sc[span[q], part] * factor_sc[set_of[q]]).astype(jnp.bfloat16)
                guess += dot(rounded, ahead_ref[weight_of[q], part])
            resid_sc[span[q]] = (target_sc[span[q]] - guess).astype(jnp.bfloat16)

    descend(True)

    @pl.loop(1, ITERS)
    def _(i):
        predict()
        descend(False)

    @pl.when(step > 0)
    def _():
        for copy in copies(step - 1)[:BAND]:
            copy.wait()

    for q in range(BAND):
        for half in range(2):
            part = slice(half * elevations, (half + 1) * elevations)
            image_sc[q, :, part] = (step_sc[span[q], part] * factor_sc[set_of[q]]).astype(
                image_sc.dtype
            )
        copies(step)[q].start()

    @pl.when(step == steps - 1)
    def _():
        if late:
            copies(step)[BAND].start()
        for copy in copies(step):
            copy.wait()


def invert(joined, targets, runs, back, ahead, out_shape, *, offset, base, edge=False, out=None, late=None):
    lines = targets.shape[0]
    steps, kinds, columns = runs.shape
    elevations = back.shape[2] // 2
    whole = pl.BlockSpec(memory_space=pltpu.VMEM)
    far = pl.BlockSpec(memory_space=pl.ANY)
    pixels = BAND * columns
    tile_width = 256
    shape = jax.ShapeDtypeStruct(out_shape, jnp.bfloat16)
    above = jax.ShapeDtypeStruct(out_shape[1:], jnp.bfloat16)
    extra = ([] if out is None else [out]) + ([] if late is None else [late])
    extra_specs = ([] if out is None else [far]) + ([] if late is None else [whole])
    return pl.pallas_call(
        functools.partial(
            band_kernel, edge=edge, base=base, held=out is not None, late=late is not None
        ),
        grid=(steps,),
        in_specs=[
            pl.BlockSpec(memory_space=pltpu.SMEM),
            pl.BlockSpec((lines, pixels), lambda i: (0, i + offset)),
            pl.BlockSpec((1, kinds, columns), lambda i: (i, 0, 0)),
            whole,
            whole,
        ]
        + extra_specs,
        out_specs=[far, far] if edge else far,
        out_shape=[shape, above] if edge else shape,
        input_output_aliases={} if out is None else {5: 0},
        scratch_shapes=[
            pltpu.VMEM((pixels, lines), jnp.float32),
            pltpu.VMEM((pixels, lines), jnp.bfloat16),
            pltpu.VMEM((pixels, 2 * elevations), jnp.float32),
            pltpu.VMEM((2 * (elevations // tile_width), columns, tile_width), jnp.float32),
            pltpu.VMEM((2, columns, elevations), jnp.float32),
            pltpu.VMEM((BAND, columns, 2 * elevations), jnp.bfloat16),
            pltpu.SemaphoreType.DMA((BAND + 1,)),
        ],
        compiler_params=pltpu.CompilerParams(vmem_limit_bytes=40 * 1024 * 1024),
        name="invert_edge" if edge else "invert",
    )(joined, targets, runs, back, ahead, *extra)


def turned(value, step):
    count = lax.axis_size("acq")
    return lax.ppermute(value, "acq", [(i, (i + step) % count) for i in range(count)])


def steering_of(phase):
    scale = 1.0 / math.sqrt(phase.shape[1])
    real = (jnp.cos(phase) * scale).astype(jnp.bfloat16)
    imag = (jnp.sin(phase) * scale).astype(jnp.bfloat16)
    return jnp.concatenate([real, imag], axis=1)


def planes_of(steering, acqs):
    count, lines, elevations = steering.shape
    real, imag = steering[:, : lines // 2], steering[:, lines // 2 :]
    upper = jnp.concatenate([real, -imag], axis=2).reshape(count, -1, 1, acqs, 2 * elevations)
    lower = jnp.concatenate([imag, real], axis=2).reshape(count, -1, 1, acqs, 2 * elevations)
    return jnp.concatenate([upper, lower], axis=2).reshape(count, lines, 2 * elevations)


def program(measurements, tile_order, steer_phase, group_ids):
    acqs = measurements.shape[0]
    rows, columns = group_ids.shape
    elevations = steer_phase.shape[2]
    assert rows % BAND == 0
    bands = rows // BAND
    edge = [rows - 1] + list(range(BAND - 1))
    inner = [list(range(BAND * b - 1, BAND * b + 2)) for b in range(1, bands)]
    early = 1
    spans = [edge + sum(inner[:early], []), sum(inner[early:], [])]
    sent = order_tiles(measurements, tile_order, spans, (rows - 1,))
    head = lax.all_to_all(sent[0], "acq", 0, 0, tiled=True)
    tail = lax.all_to_all(sent[1], "acq", 0, 0, tiled=True)
    mine = steering_of(steer_phase)
    before = turned(mine, 1)
    back = planes_of(jnp.concatenate([before, mine], axis=0), acqs)
    ahead = back.transpose(0, 2, 1)
    back = back * STEP_SIZE
    runs = (group_ids % columns + BAND - 1) // BAND
    first = lax.axis_index("acq") == 0
    column = jnp.arange(columns, dtype=jnp.int32)
    turn = (columns - 1) % BAND
    last_starts = jnp.maximum(0, BAND * ((column - turn + BAND) // BAND) - BAND + turn)
    last_runs = (last_starts + BAND - 1) // BAND
    edge_runs = jnp.stack([jnp.where(first, last_runs, runs[0]), runs[0]])[None]
    inner_runs = runs[BAND - 1 : rows - 1 : BAND][:, None]
    joined = jnp.where(first, 0, 1).reshape(1)
    shape = (rows, columns, 2 * elevations)
    out, above = invert(joined, head, edge_runs, back, ahead, shape, offset=0, base=0, edge=True)
    late = turned(above, -1)
    out = invert(joined, head, inner_runs[:early], back, ahead, shape, offset=1, base=1, out=out)
    out = invert(
        joined, tail, inner_runs[early:-1], back, ahead, shape,
        offset=0, base=1 + early, out=out,
    )
    return invert(
        joined, tail, inner_runs[-1:], back, ahead, shape,
        offset=bands - 2 - early, base=bands - 1, out=out, late=late,
    )


def solution(mesh):
    placed = (
        P(("groups", "acq"), None, None, None, None),
        P("groups"),
        P(("groups", "acq"), None, None),
        P(("groups", "acq"), None),
    )
    return jax.shard_map(
        program,
        mesh=mesh,
        in_specs=placed,
        out_specs=P(("groups", "acq"), None, None),
        check_vma=False,
    )
```

```python
import functools
import math

import jax
import jax.numpy as jnp
from jax import lax
from jax.experimental import pallas as pl
from jax.experimental.pallas import tpu as pltpu
from jax.sharding import PartitionSpec as P


ITERS = 3
BAND = 3
STEP_SIZE = 0.0625
SHRINK_LEVEL = 3.0


def dot(a, b, dims=((1,), (0,))):
    return lax.dot_general(a, b, (dims, ((), ())), preferred_element_type=jnp.float32)


def order_kernel(order_ref, *refs, spans, ahead_rows):
    stack_ref, sent_refs = refs[0], refs[1:]
    acqs, parts, _, tiles, columns = stack_ref.shape
    lines = acqs * parts * tiles
    share = acqs * parts
    target = lax.broadcasted_iota(jnp.int32, (lines, 1), 0)
    source = lax.broadcasted_iota(jnp.int32, (1, lines), 1)
    block = lax.rem(source, tiles)
    part = lax.rem(lax.div(source, tiles), parts)
    acq = lax.div(source, tiles * parts)
    tile = jnp.zeros((1, lines), jnp.int32)
    for k in range(tiles):
        tile = jnp.where(block == k, order_ref[k], tile)
    after = jnp.where(tile == tiles - 1, 0, tile + 1)
    inner = part * acqs + acq
    pick = jnp.where(target == tile * share + inner, 1.0, 0.0).astype(jnp.bfloat16)
    pick_after = jnp.where(target == after * share + inner, 1.0, 0.0).astype(jnp.bfloat16)
    for sent_ref, span in zip(sent_refs, spans):
        for q, row in enumerate(span):
            lump = stack_ref[:, :, row].reshape(lines, columns)
            chosen = pick_after if row in ahead_rows else pick
            sent_ref[:, q * columns : (q + 1) * columns] = dot(chosen, lump).astype(sent_ref.dtype)


def order_tiles(measurements, tile_order, spans, ahead_rows):
    acqs, parts, tiles, _, columns = measurements.shape
    stack = measurements.transpose(0, 1, 3, 2, 4)
    lines = acqs * parts * tiles
    whole = pl.BlockSpec(memory_space=pltpu.VMEM)
    return pl.pallas_call(
        functools.partial(order_kernel, spans=spans, ahead_rows=ahead_rows),
        in_specs=[pl.BlockSpec(memory_space=pltpu.SMEM), whole],
        out_specs=[whole] * len(spans),
        out_shape=[
            jax.ShapeDtypeStruct((lines, len(span) * columns), measurements.dtype) for span in spans
        ],
        name="order_tiles",
    )(tile_order, stack)


def run_sums(energy, pick):
    return dot(pick, energy.astype(jnp.bfloat16))


def shrink_factor(sums, pick):
    factor = jnp.maximum(1.0 - SHRINK_LEVEL * lax.rsqrt(jnp.maximum(sums, SHRINK_LEVEL**2)), 0.0)
    high = factor.astype(jnp.bfloat16)
    low = (factor - high.astype(jnp.float32)).astype(jnp.bfloat16)
    both = jnp.concatenate([high, low], axis=0)
    return dot(jnp.concatenate([pick, pick], axis=0), both, ((0,), (0,)))


def band_kernel(joined_ref, target_ref, run_ref, *refs, edge, base, held):
    refs = list(refs)
    back_refs = [refs.pop(0) for _ in range(2 if edge else 1)]
    ahead_refs = [refs.pop(0) for _ in range(2 if edge else 1)]
    if held:
        refs.pop(0)
    out_ref = refs.pop(0)
    above_ref = refs.pop(0) if edge else None
    target_sc, resid_sc, step_sc, energy_sc, factor_sc, image_sc, sem = refs
    step = pl.program_id(0)
    steps = pl.num_programs(0)
    columns = run_ref.shape[2]
    elevations = factor_sc.shape[2]
    tile_width = energy_sc.shape[2]
    groups = -(-(columns // BAND + 2) // 16) * 16
    weight_of = (0,) + (len(back_refs) - 1,) * (BAND - 1)
    set_of = (0 if edge else 1,) + (1,) * (BAND - 1)
    span = [slice(q * columns, (q + 1) * columns) for q in range(BAND)]

    def copies(of):
        first = BAND * (base + of) - 1
        targets = [above_ref if edge and q == 0 else out_ref.at[first + q] for q in range(BAND)]
        return [pltpu.make_async_copy(image_sc.at[q], targets[q], sem.at[q]) for q in range(BAND)]

    group = lax.broadcasted_iota(jnp.int32, (groups, columns), 0)
    picks = [
        jnp.where(group == run_ref[0, n : n + 1], 1.0, 0.0).astype(jnp.bfloat16)
        for n in range(run_ref.shape[1])
    ]
    target_sc[...] = target_ref[...].T

    def descend(is_first):
        for at in range(0, elevations, tile_width):
            real = slice(at, at + tile_width)
            imag = slice(elevations + at, elevations + at + tile_width)
            for q in range(BAND):
                if is_first:
                    resid = target_sc[span[q]]
                else:
                    resid = resid_sc[span[q]]
                step_real = dot(resid, back_refs[weight_of[q]][:, real])
                step_imag = dot(resid, back_refs[weight_of[q]][:, imag])
                if not is_first:
                    factor = factor_sc[set_of[q], :, real]
                    step_real += step_sc[span[q], real] * factor
                    step_imag += step_sc[span[q], imag] * factor
                step_sc[span[q], real] = step_real
                step_sc[span[q], imag] = step_imag
                energy = step_real * step_real + step_imag * step_imag
                slot = 2 * (at // tile_width) + set_of[q]
                if q > 0 and set_of[q] == set_of[q - 1]:
                    energy += energy_sc[slot]
                energy_sc[slot] = energy

        for at in range(0, elevations, tile_width):
            real = slice(at, at + tile_width)
            slot = 2 * (at // tile_width)
            sums = run_sums(energy_sc[slot + 1], picks[-1])
            if edge:
                apart = run_sums(energy_sc[slot], picks[0])
                joined = joined_ref[0] > 0
                factor_sc[0, :, real] = shrink_factor(
                    jnp.where(joined, apart + sums, apart), picks[0]
                )
                sums = jnp.where(joined, apart + sums, sums)
            factor_sc[1, :, real] = shrink_factor(sums, picks[-1])

    def predict():
        for q in range(BAND):
            guess = jnp.zeros((columns, target_sc.shape[1]), jnp.float32)
            for half in range(2):
                part = slice(half * elevations, (half + 1) * elevations)
                rounded = (step_sc[span[q], part] * factor_sc[set_of[q]]).astype(jnp.bfloat16)
                guess += dot(rounded, ahead_refs[weight_of[q]][part])
            resid_sc[span[q]] = (target_sc[span[q]].astype(jnp.float32) - guess).astype(
                jnp.bfloat16
            )

    descend(True)

    @pl.loop(1, ITERS)
    def _(i):
        predict()
        descend(False)

    @pl.when(step > 0)
    def _():
        for copy in copies(step - 1):
            copy.wait()

    for q in range(BAND):
        for half in range(2):
            part = slice(half * elevations, (half + 1) * elevations)
            image_sc[q, :, part] = (step_sc[span[q], part] * factor_sc[set_of[q]]).astype(
                image_sc.dtype
            )
        copies(step)[q].start()

    @pl.when(step == steps - 1)
    def _():
        for copy in copies(step):
            copy.wait()


def invert(joined, targets, runs, backs, aheads, out_shape, *, offset, base, edge=False, out=None):
    lines = targets.shape[0]
    steps, kinds, columns = runs.shape
    elevations = backs[0].shape[1] // 2
    whole = pl.BlockSpec(memory_space=pltpu.VMEM)
    far = pl.BlockSpec(memory_space=pl.ANY)
    pixels = BAND * columns
    tile_width = 256
    shape = jax.ShapeDtypeStruct(out_shape, jnp.bfloat16)
    above = jax.ShapeDtypeStruct(out_shape[1:], jnp.bfloat16)
    weights = [*backs, *aheads]
    extra = [] if out is None else [out]
    return pl.pallas_call(
        functools.partial(band_kernel, edge=edge, base=base, held=out is not None),
        grid=(steps,),
        in_specs=[
            pl.BlockSpec(memory_space=pltpu.SMEM),
            pl.BlockSpec((lines, pixels), lambda i: (0, i + offset)),
            pl.BlockSpec((1, kinds, columns), lambda i: (i, 0, 0)),
        ]
        + [whole] * len(weights)
        + [far] * len(extra),
        out_specs=[far, far] if edge else far,
        out_shape=[shape, above] if edge else shape,
        input_output_aliases={} if out is None else {3 + len(weights): 0},
        scratch_shapes=[
            pltpu.VMEM((pixels, lines), jnp.bfloat16),
            pltpu.VMEM((pixels, lines), jnp.bfloat16),
            pltpu.VMEM((pixels, 2 * elevations), jnp.float32),
            pltpu.VMEM((2 * (elevations // tile_width), columns, tile_width), jnp.float32),
            pltpu.VMEM((2, columns, elevations), jnp.float32),
            pltpu.VMEM((BAND, columns, 2 * elevations), jnp.bfloat16),
            pltpu.SemaphoreType.DMA((BAND,)),
        ],
        compiler_params=pltpu.CompilerParams(vmem_limit_bytes=40 * 1024 * 1024),
        name="invert_edge" if edge else "invert",
    )(joined, targets, runs, *weights, *extra)


def place_kernel(row_ref, _, out_ref, sem):
    copy = pltpu.make_async_copy(row_ref, out_ref.at[out_ref.shape[0] - 1], sem)
    copy.start()
    copy.wait()


def place_last_row(row, out):
    far = pl.BlockSpec(memory_space=pl.ANY)
    return pl.pallas_call(
        place_kernel,
        in_specs=[pl.BlockSpec(memory_space=pltpu.VMEM), far],
        out_specs=far,
        out_shape=jax.ShapeDtypeStruct(out.shape, out.dtype),
        input_output_aliases={1: 0},
        scratch_shapes=[pltpu.SemaphoreType.DMA],
        compiler_params=pltpu.CompilerParams(vmem_limit_bytes=4 * 1024 * 1024),
        name="place_last_row",
    )(row, out)


def turned(value, step):
    count = lax.axis_size("acq")
    return lax.ppermute(value, "acq", [(i, (i + step) % count) for i in range(count)])


def steering_of(phase):
    scale = 1.0 / math.sqrt(phase.shape[1])
    real = (jnp.cos(phase) * scale).astype(jnp.bfloat16)
    imag = (jnp.sin(phase) * scale).astype(jnp.bfloat16)
    return jnp.concatenate([real, imag], axis=1)


def planes_of(steering, acqs):
    _, lines, elevations = steering.shape
    real, imag = steering[0, : lines // 2], steering[0, lines // 2 :]
    upper = jnp.concatenate([real, -imag], axis=1).reshape(-1, 1, acqs, 2 * elevations)
    lower = jnp.concatenate([imag, real], axis=1).reshape(-1, 1, acqs, 2 * elevations)
    plane = jnp.concatenate([upper, lower], axis=1).reshape(lines, 2 * elevations)
    return plane * STEP_SIZE, plane.T


def program(measurements, tile_order, steer_phase, group_ids):
    acqs = measurements.shape[0]
    rows, columns = group_ids.shape
    elevations = steer_phase.shape[2]
    assert rows % BAND == 0
    bands = rows // BAND
    edge = [rows - 1] + list(range(BAND - 1))
    inner = [list(range(BAND * b - 1, BAND * b + 2)) for b in range(1, bands)]
    early = 1
    spans = [edge + sum(inner[:early], []), sum(inner[early:], [])]
    sent = order_tiles(measurements, tile_order, spans, (rows - 1,))
    head = lax.all_to_all(sent[0], "acq", 0, 0, tiled=True)
    tail = lax.all_to_all(sent[1], "acq", 0, 0, tiled=True)
    mine = steering_of(steer_phase)
    before = turned(mine, 1)
    back, ahead = planes_of(mine, acqs)
    back_before, ahead_before = planes_of(before, acqs)
    runs = (group_ids % columns + BAND - 1) // BAND
    first = lax.axis_index("acq") == 0
    column = jnp.arange(columns, dtype=jnp.int32)
    turn = (columns - 1) % BAND
    last_starts = jnp.maximum(0, BAND * ((column - turn + BAND) // BAND) - BAND + turn)
    last_runs = (last_starts + BAND - 1) // BAND
    edge_runs = jnp.stack([jnp.where(first, last_runs, runs[0]), runs[0]])[None]
    inner_runs = runs[BAND - 1 : rows - 1 : BAND][:, None]
    joined = jnp.where(first, 0, 1).reshape(1)
    shape = (rows, columns, 2 * elevations)
    out = invert(
        joined, head, inner_runs[:early], [back], [ahead], shape, offset=1, base=1
    )
    out, above = invert(
        joined, head, edge_runs, [back_before, back], [ahead_before, ahead], shape,
        offset=0, base=0, edge=True, out=out,
    )
    late = turned(above, -1)
    out = invert(
        joined, tail, inner_runs[early:], [back], [ahead], shape,
        offset=0, base=1 + early, out=out,
    )
    return place_last_row(late, out)


def solution(mesh):
    placed = (
        P(("groups", "acq"), None, None, None, None),
        P("groups"),
        P(("groups", "acq"), None, None),
        P(("groups", "acq"), None),
    )
    return jax.shard_map(
        program,
        mesh=mesh,
        in_specs=placed,
        out_specs=P(("groups", "acq"), None, None),
        check_vma=False,
    )
```

```python
import functools
import math

import jax
import jax.numpy as jnp
from jax import lax
from jax.experimental import pallas as pl
from jax.experimental.pallas import tpu as pltpu
from jax.sharding import PartitionSpec as P


ITERS = 3
BAND = 3
STEP_SIZE = 0.0625
SHRINK_LEVEL = 3.0


def dot(a, b, dims=((1,), (0,))):
    return lax.dot_general(a, b, (dims, ((), ())), preferred_element_type=jnp.float32)


def pieces_of(span):
    pieces = []
    for place, row in enumerate(span):
        if pieces and row == pieces[-1][0] + pieces[-1][1]:
            pieces[-1][1] += 1
        else:
            pieces.append([row, 1, place])
    return pieces


def order_kernel(order_ref, stack_ref, sent_ref, rows_sc, sem, *, span, ahead_rows):
    acqs, parts, _, tiles, columns = rows_sc.shape
    copies = [
        pltpu.make_async_copy(
            stack_ref.at[:, :, pl.ds(row, count)], rows_sc.at[:, :, pl.ds(place, count)], sem.at[n]
        )
        for n, (row, count, place) in enumerate(pieces_of(span))
    ]
    for copy in copies:
        copy.start()
    lines = acqs * parts * tiles
    share = acqs * parts
    target = lax.broadcasted_iota(jnp.int32, (lines, 1), 0)
    source = lax.broadcasted_iota(jnp.int32, (1, lines), 1)
    block = lax.rem(source, tiles)
    part = lax.rem(lax.div(source, tiles), parts)
    acq = lax.div(source, tiles * parts)
    tile = jnp.zeros((1, lines), jnp.int32)
    for k in range(tiles):
        tile = jnp.where(block == k, order_ref[k], tile)
    after = jnp.where(tile == tiles - 1, 0, tile + 1)
    inner = part * acqs + acq
    pick = jnp.where(target == tile * share + inner, 1.0, 0.0).astype(jnp.bfloat16)
    pick_after = jnp.where(target == after * share + inner, 1.0, 0.0).astype(jnp.bfloat16)
    for copy in copies:
        copy.wait()
    for q, row in enumerate(span):
        lump = rows_sc[:, :, q].reshape(lines, columns)
        chosen = pick_after if row in ahead_rows else pick
        sent_ref[:, q * columns : (q + 1) * columns] = dot(chosen, lump).astype(sent_ref.dtype)


def order_tiles(measurements, tile_order, span, ahead_rows):
    acqs, parts, tiles, _, columns = measurements.shape
    stack = measurements.transpose(0, 1, 3, 2, 4)
    lines = acqs * parts * tiles
    return pl.pallas_call(
        functools.partial(order_kernel, span=span, ahead_rows=ahead_rows),
        in_specs=[pl.BlockSpec(memory_space=pltpu.SMEM), pl.BlockSpec(memory_space=pl.ANY)],
        out_specs=pl.BlockSpec(memory_space=pltpu.VMEM),
        out_shape=jax.ShapeDtypeStruct((lines, len(span) * columns), measurements.dtype),
        scratch_shapes=[
            pltpu.VMEM((acqs, parts, len(span), tiles, columns), measurements.dtype),
            pltpu.SemaphoreType.DMA((len(pieces_of(span)),)),
        ],
        name="order_tiles",
    )(tile_order, stack)


def run_sums(energy, pick):
    return dot(pick, energy.astype(jnp.bfloat16))


def shrink_factor(sums, pick):
    factor = jnp.maximum(1.0 - SHRINK_LEVEL * lax.rsqrt(jnp.maximum(sums, SHRINK_LEVEL**2)), 0.0)
    high = factor.astype(jnp.bfloat16)
    low = (factor - high.astype(jnp.float32)).astype(jnp.bfloat16)
    both = jnp.concatenate([high, low], axis=0)
    return dot(jnp.concatenate([pick, pick], axis=0), both, ((0,), (0,)))


def band_kernel(active_ref, *refs, edge, apart, base, held):
    settings = dict(edge=edge, apart=apart, base=base, held=held)
    if not edge:
        return band_body(*refs, **settings)

    @pl.when(active_ref[0] > 0)
    def _():
        band_body(*refs, **settings)


def band_body(target_ref, run_ref, *refs, edge, apart, base, held):
    refs = list(refs)
    back_refs = [refs.pop(0) for _ in range(2 if edge else 1)]
    ahead_refs = [refs.pop(0) for _ in range(2 if edge else 1)]
    if held:
        refs.pop(0)
    out_ref = refs.pop(0)
    above_ref = refs.pop(0) if edge else None
    target_sc, resid_sc, step_sc, past_sc, energy_sc, factor_sc, image_sc, sem = refs
    step = pl.program_id(0)
    steps = pl.num_programs(0)
    columns = run_ref.shape[2]
    elevations = factor_sc.shape[2]
    tile_width = energy_sc.shape[2]
    groups = -(-(columns // BAND + 2) // 16) * 16
    weight_of = (0,) + (len(back_refs) - 1,) * (BAND - 1)
    set_of = (0 if apart else 1,) + (1,) * (BAND - 1)
    span = [slice(q * columns, (q + 1) * columns) for q in range(BAND)]

    def copies(of):
        first = BAND * (base + of) - 1
        targets = [above_ref if edge and q == 0 else out_ref.at[first + q] for q in range(BAND)]
        return [pltpu.make_async_copy(image_sc.at[q], targets[q], sem.at[q]) for q in range(BAND)]

    group = lax.broadcasted_iota(jnp.int32, (groups, columns), 0)
    picks = [
        jnp.where(group == run_ref[0, n : n + 1], 1.0, 0.0).astype(jnp.bfloat16)
        for n in range(run_ref.shape[1])
    ]
    target_sc[...] = target_ref[...].T

    def descend(is_first):
        for at in range(0, elevations, tile_width):
            real = slice(at, at + tile_width)
            imag = slice(elevations + at, elevations + at + tile_width)
            for q in range(BAND):
                if is_first:
                    resid = target_sc[span[q]]
                else:
                    resid = resid_sc[span[q]]
                step_real = dot(resid, back_refs[weight_of[q]][:, real])
                step_imag = dot(resid, back_refs[weight_of[q]][:, imag])
                if not is_first:
                    step_real += past_sc[span[q], real]
                    step_imag += past_sc[span[q], imag]
                step_sc[span[q], real] = step_real
                step_sc[span[q], imag] = step_imag
                energy = step_real * step_real + step_imag * step_imag
                slot = 2 * (at // tile_width) + set_of[q]
                if q > 0 and set_of[q] == set_of[q - 1]:
                    energy += energy_sc[slot]
                energy_sc[slot] = energy

        for at in range(0, elevations, tile_width):
            real = slice(at, at + tile_width)
            slot = 2 * (at // tile_width)
            sums = run_sums(energy_sc[slot + 1], picks[-1])
            if apart:
                alone = run_sums(energy_sc[slot], picks[0])
                factor_sc[0, :, real] = shrink_factor(alone, picks[0])
            factor_sc[1, :, real] = shrink_factor(sums, picks[-1])

    def predict():
        for q in range(BAND):
            guess = jnp.zeros((columns, target_sc.shape[1]), jnp.float32)
            for half in range(2):
                part = slice(half * elevations, (half + 1) * elevations)
                settled = step_sc[span[q], part] * factor_sc[set_of[q]]
                past_sc[span[q], part] = settled
                guess += dot(settled.astype(jnp.bfloat16), ahead_refs[weight_of[q]][part])
            resid_sc[span[q]] = (target_sc[span[q]].astype(jnp.float32) - guess).astype(
                jnp.bfloat16
            )

    descend(True)

    @pl.loop(1, ITERS)
    def _(i):
        predict()
        descend(False)

    @pl.when(step > 0)
    def _():
        for copy in copies(step - 1):
            copy.wait()

    for q in range(BAND):
        for half in range(2):
            part = slice(half * elevations, (half + 1) * elevations)
            image_sc[q, :, part] = (step_sc[span[q], part] * factor_sc[set_of[q]]).astype(
                image_sc.dtype
            )
        copies(step)[q].start()

    @pl.when(step == steps - 1)
    def _():
        for copy in copies(step):
            copy.wait()


def invert(active, targets, runs, backs, aheads, out_shape, *, offset, base, edge=False, apart=False, out=None):
    lines = targets.shape[0]
    steps, kinds, columns = runs.shape
    elevations = backs[0].shape[1] // 2
    whole = pl.BlockSpec(memory_space=pltpu.VMEM)
    far = pl.BlockSpec(memory_space=pl.ANY)
    pixels = BAND * columns
    tile_width = 256
    shape = jax.ShapeDtypeStruct(out_shape, jnp.bfloat16)
    above = jax.ShapeDtypeStruct(out_shape[1:], jnp.bfloat16)
    weights = [*backs, *aheads]
    extra = [] if out is None else [out]
    return pl.pallas_call(
        functools.partial(
            band_kernel, edge=edge, apart=apart, base=base, held=out is not None
        ),
        grid=(steps,),
        in_specs=[
            pl.BlockSpec(memory_space=pltpu.SMEM),
            pl.BlockSpec((lines, pixels), lambda i: (0, i + offset)),
            pl.BlockSpec((1, kinds, columns), lambda i: (i, 0, 0)),
        ]
        + [whole] * len(weights)
        + [far] * len(extra),
        out_specs=[far, far] if edge else far,
        out_shape=[shape, above] if edge else shape,
        input_output_aliases={} if out is None else {3 + len(weights): 0},
        scratch_shapes=[
            pltpu.VMEM((pixels, lines), jnp.bfloat16),
            pltpu.VMEM((pixels, lines), jnp.bfloat16),
            pltpu.VMEM((pixels, 2 * elevations), jnp.float32),
            pltpu.VMEM((pixels, 2 * elevations), jnp.float32),
            pltpu.VMEM((2 * (elevations // tile_width), columns, tile_width), jnp.float32),
            pltpu.VMEM((2, columns, elevations), jnp.float32),
            pltpu.VMEM((BAND, columns, 2 * elevations), jnp.bfloat16),
            pltpu.SemaphoreType.DMA((BAND,)),
        ],
        compiler_params=pltpu.CompilerParams(vmem_limit_bytes=40 * 1024 * 1024),
        name="invert_apart" if apart else "invert_edge" if edge else "invert",
    )(active, targets, runs, *weights, *extra)


def place_kernel(last_ref, row_ref, last_row_ref, _, out_ref, sem):
    target = out_ref.at[out_ref.shape[0] - 1]

    @pl.when(last_ref[0] > 0)
    def _():
        copy = pltpu.make_async_copy(last_row_ref, target, sem)
        copy.start()
        copy.wait()

    @pl.when(last_ref[0] == 0)
    def _():
        copy = pltpu.make_async_copy(row_ref, target, sem)
        copy.start()
        copy.wait()


def place_last_row(is_last, row, last_row, out):
    far = pl.BlockSpec(memory_space=pl.ANY)
    whole = pl.BlockSpec(memory_space=pltpu.VMEM)
    return pl.pallas_call(
        place_kernel,
        in_specs=[pl.BlockSpec(memory_space=pltpu.SMEM), whole, whole, far],
        out_specs=far,
        out_shape=jax.ShapeDtypeStruct(out.shape, out.dtype),
        input_output_aliases={3: 0},
        scratch_shapes=[pltpu.SemaphoreType.DMA],
        compiler_params=pltpu.CompilerParams(vmem_limit_bytes=4 * 1024 * 1024),
        name="place_last_row",
    )(is_last, row, last_row, out)


def turned(value, step):
    count = lax.axis_size("acq")
    return lax.ppermute(value, "acq", [(i, (i + step) % count) for i in range(count)])


def steering_of(phase):
    scale = 1.0 / math.sqrt(phase.shape[1])
    real = (jnp.cos(phase) * scale).astype(jnp.bfloat16)
    imag = (jnp.sin(phase) * scale).astype(jnp.bfloat16)
    return jnp.concatenate([real, imag], axis=1)


def planes_of(steering, acqs):
    _, lines, elevations = steering.shape
    real, imag = steering[0, : lines // 2], steering[0, lines // 2 :]
    upper = jnp.concatenate([real, -imag], axis=1).reshape(-1, 1, acqs, 2 * elevations)
    lower = jnp.concatenate([imag, real], axis=1).reshape(-1, 1, acqs, 2 * elevations)
    plane = jnp.concatenate([upper, lower], axis=1).reshape(lines, 2 * elevations)
    return plane * STEP_SIZE, plane.T


def program(measurements, tile_order, steer_phase, group_ids):
    acqs = measurements.shape[0]
    rows, columns = group_ids.shape
    elevations = steer_phase.shape[2]
    assert rows % BAND == 0
    bands = rows // BAND
    edge = [rows - 1] + list(range(BAND - 1))
    inner = [list(range(BAND * b - 1, BAND * b + 2)) for b in range(1, bands)]
    early = 1
    spans = [edge + sum(inner[:early], []), sum(inner[early:], [])]
    sent = order_tiles(measurements, tile_order, spans[0], (rows - 1,))
    head = lax.all_to_all(sent, "acq", 0, 0, tiled=True)
    sent = order_tiles(measurements, tile_order, spans[1], ())
    tail = lax.all_to_all(sent, "acq", 0, 0, tiled=True)
    mine = steering_of(steer_phase)
    before = turned(mine, 1)
    back, ahead = planes_of(mine, acqs)
    back_before, ahead_before = planes_of(before, acqs)
    runs = (group_ids % columns + BAND - 1) // BAND
    first = lax.axis_index("acq") == 0
    column = jnp.arange(columns, dtype=jnp.int32)
    turn = (columns - 1) % BAND
    last_starts = jnp.maximum(0, BAND * ((column - turn + BAND) // BAND) - BAND + turn)
    last_runs = (last_starts + BAND - 1) // BAND
    apart_runs = jnp.stack([last_runs, runs[0]])[None]
    inner_runs = runs[BAND - 1 : rows - 1 : BAND][:, None]
    count = lax.axis_size("acq")
    is_first = jnp.where(first, 1, 0).reshape(1)
    is_last = jnp.where(lax.axis_index("acq") == count - 1, 1, 0).reshape(1)
    shape = (rows, columns, 2 * elevations)
    out = invert(
        is_first, head, inner_runs[:early], [back], [ahead], shape, offset=1, base=1
    )
    sides = dict(offset=0, base=0, edge=True)
    both = [back_before, back], [ahead_before, ahead]
    out, above = invert(is_first, head, apart_runs, *both, shape, apart=True, out=out, **sides)
    last_row = lax.ppermute(above, "acq", [(0, count - 1)])
    out, above = invert(1 - is_first, head, runs[:1][None], *both, shape, out=out, **sides)
    row = lax.ppermute(above, "acq", [(i, i - 1) for i in range(1, count)])
    out = invert(
        is_first, tail, inner_runs[early:], [back], [ahead], shape,
        offset=0, base=1 + early, out=out,
    )
    return place_last_row(is_last, row, last_row, out)


def solution(mesh):
    placed = (
        P(("groups", "acq"), None, None, None, None),
        P("groups"),
        P(("groups", "acq"), None, None),
        P(("groups", "acq"), None),
    )
    return jax.shard_map(
        program,
        mesh=mesh,
        in_specs=placed,
        out_specs=P(("groups", "acq"), None, None),
        check_vma=False,
    )
```

```python
import functools
import math

import jax
import jax.numpy as jnp
from jax import lax
from jax.experimental import pallas as pl
from jax.experimental.pallas import tpu as pltpu
from jax.sharding import PartitionSpec as P


ITERS = 3
BAND = 3
STEP_SIZE = 0.0625
SHRINK_LEVEL = 3.0


def dot(a, b, dims=((1,), (0,))):
    return lax.dot_general(a, b, (dims, ((), ())), preferred_element_type=jnp.float32)


def order_kernel(order_ref, *refs, spans, ahead_rows):
    stack_ref, sent_refs = refs[0], refs[1:]
    acqs, parts, _, tiles, columns = stack_ref.shape
    lines = acqs * parts * tiles
    share = acqs * parts
    target = lax.broadcasted_iota(jnp.int32, (lines, 1), 0)
    source = lax.broadcasted_iota(jnp.int32, (1, lines), 1)
    block = lax.rem(source, tiles)
    part = lax.rem(lax.div(source, tiles), parts)
    acq = lax.div(source, tiles * parts)
    tile = jnp.zeros((1, lines), jnp.int32)
    for k in range(tiles):
        tile = jnp.where(block == k, order_ref[k], tile)
    after = jnp.where(tile == tiles - 1, 0, tile + 1)
    inner = part * acqs + acq
    pick = jnp.where(target == tile * share + inner, 1.0, 0.0).astype(jnp.bfloat16)
    pick_after = jnp.where(target == after * share + inner, 1.0, 0.0).astype(jnp.bfloat16)
    for sent_ref, span in zip(sent_refs, spans):
        for q, row in enumerate(span):
            lump = stack_ref[:, :, row].reshape(lines, columns)
            chosen = pick_after if row in ahead_rows else pick
            sent_ref[:, q * columns : (q + 1) * columns] = dot(chosen, lump).astype(sent_ref.dtype)


def order_tiles(measurements, tile_order, spans, ahead_rows):
    acqs, parts, tiles, _, columns = measurements.shape
    stack = measurements.transpose(0, 1, 3, 2, 4)
    lines = acqs * parts * tiles
    whole = pl.BlockSpec(memory_space=pltpu.VMEM)
    return pl.pallas_call(
        functools.partial(order_kernel, spans=spans, ahead_rows=ahead_rows),
        in_specs=[pl.BlockSpec(memory_space=pltpu.SMEM), whole],
        out_specs=[whole] * len(spans),
        out_shape=[
            jax.ShapeDtypeStruct((lines, len(span) * columns), measurements.dtype) for span in spans
        ],
        name="order_tiles",
    )(tile_order, stack)


def run_sums(energy, pick):
    return dot(pick, energy.astype(jnp.bfloat16))


def shrink_factor(sums, pick):
    factor = jnp.maximum(1.0 - SHRINK_LEVEL * lax.rsqrt(jnp.maximum(sums, SHRINK_LEVEL**2)), 0.0)
    high = factor.astype(jnp.bfloat16)
    low = (factor - high.astype(jnp.float32)).astype(jnp.bfloat16)
    both = jnp.concatenate([high, low], axis=0)
    return dot(jnp.concatenate([pick, pick], axis=0), both, ((0,), (0,)))


def band_kernel(active_ref, *refs, edge, apart, base, held):
    settings = dict(edge=edge, apart=apart, base=base, held=held)
    if not edge:
        return band_body(*refs, **settings)

    @pl.when(active_ref[0] > 0)
    def _():
        band_body(*refs, **settings)


def band_body(target_ref, run_ref, *refs, edge, apart, base, held):
    refs = list(refs)
    back_refs = [refs.pop(0) for _ in range(2 if edge else 1)]
    ahead_refs = [refs.pop(0) for _ in range(2 if edge else 1)]
    if held:
        refs.pop(0)
    out_ref = refs.pop(0)
    above_ref = refs.pop(0) if edge else None
    target_sc, resid_sc, step_sc, past_sc, energy_sc, factor_sc, image_sc, sem = refs
    step = pl.program_id(0)
    steps = pl.num_programs(0)
    columns = run_ref.shape[2]
    elevations = factor_sc.shape[2]
    tile_width = energy_sc.shape[2]
    groups = -(-(columns // BAND + 2) // 16) * 16
    weight_of = (0,) + (len(back_refs) - 1,) * (BAND - 1)
    set_of = (0 if apart else 1,) + (1,) * (BAND - 1)
    span = [slice(q * columns, (q + 1) * columns) for q in range(BAND)]

    def copies(of):
        first = BAND * (base + of) - 1
        targets = [above_ref if edge and q == 0 else out_ref.at[first + q] for q in range(BAND)]
        return [pltpu.make_async_copy(image_sc.at[q], targets[q], sem.at[q]) for q in range(BAND)]

    group = lax.broadcasted_iota(jnp.int32, (groups, columns), 0)
    picks = [
        jnp.where(group == run_ref[0, n : n + 1], 1.0, 0.0).astype(jnp.bfloat16)
        for n in range(run_ref.shape[1])
    ]
    target_sc[...] = target_ref[...].T

    def descend(is_first):
        for at in range(0, elevations, tile_width):
            real = slice(at, at + tile_width)
            imag = slice(elevations + at, elevations + at + tile_width)
            for q in range(BAND):
                if is_first:
                    resid = target_sc[span[q]]
                else:
                    resid = resid_sc[span[q]]
                step_real = dot(resid, back_refs[weight_of[q]][:, real])
                step_imag = dot(resid, back_refs[weight_of[q]][:, imag])
                if not is_first:
                    step_real += past_sc[span[q], real]
                    step_imag += past_sc[span[q], imag]
                step_sc[span[q], real] = step_real
                step_sc[span[q], imag] = step_imag
                energy = step_real * step_real + step_imag * step_imag
                slot = 2 * (at // tile_width) + set_of[q]
                if q > 0 and set_of[q] == set_of[q - 1]:
                    energy += energy_sc[slot]
                energy_sc[slot] = energy

        for at in range(0, elevations, tile_width):
            real = slice(at, at + tile_width)
            slot = 2 * (at // tile_width)
            sums = run_sums(energy_sc[slot + 1], picks[-1])
            if apart:
                alone = run_sums(energy_sc[slot], picks[0])
                factor_sc[0, :, real] = shrink_factor(alone, picks[0])
            factor_sc[1, :, real] = shrink_factor(sums, picks[-1])

    def predict():
        for q in range(BAND):
            guess = jnp.zeros((columns, target_sc.shape[1]), jnp.float32)
            for half in range(2):
                part = slice(half * elevations, (half + 1) * elevations)
                settled = step_sc[span[q], part] * factor_sc[set_of[q]]
                past_sc[span[q], part] = settled
                guess += dot(settled.astype(jnp.bfloat16), ahead_refs[weight_of[q]][part])
            resid_sc[span[q]] = (target_sc[span[q]].astype(jnp.float32) - guess).astype(
                jnp.bfloat16
            )

    descend(True)

    @pl.loop(1, ITERS)
    def _(i):
        predict()
        descend(False)

    @pl.when(step > 0)
    def _():
        for copy in copies(step - 1):
            copy.wait()

    for q in range(BAND):
        for half in range(2):
            part = slice(half * elevations, (half + 1) * elevations)
            image_sc[q, :, part] = (step_sc[span[q], part] * factor_sc[set_of[q]]).astype(
                image_sc.dtype
            )
        copies(step)[q].start()

    @pl.when(step == steps - 1)
    def _():
        for copy in copies(step):
            copy.wait()


def invert(active, targets, runs, backs, aheads, out_shape, *, offset, base, edge=False, apart=False, out=None):
    lines = targets.shape[0]
    steps, kinds, columns = runs.shape
    elevations = backs[0].shape[1] // 2
    whole = pl.BlockSpec(memory_space=pltpu.VMEM)
    far = pl.BlockSpec(memory_space=pl.ANY)
    pixels = BAND * columns
    tile_width = 256
    shape = jax.ShapeDtypeStruct(out_shape, jnp.bfloat16)
    above = jax.ShapeDtypeStruct(out_shape[1:], jnp.bfloat16)
    weights = [*backs, *aheads]
    extra = [] if out is None else [out]
    return pl.pallas_call(
        functools.partial(
            band_kernel, edge=edge, apart=apart, base=base, held=out is not None
        ),
        grid=(steps,),
        in_specs=[
            pl.BlockSpec(memory_space=pltpu.SMEM),
            pl.BlockSpec((lines, pixels), lambda i: (0, i + offset)),
            pl.BlockSpec((1, kinds, columns), lambda i: (i, 0, 0)),
        ]
        + [whole] * len(weights)
        + [far] * len(extra),
        out_specs=[far, far] if edge else far,
        out_shape=[shape, above] if edge else shape,
        input_output_aliases={} if out is None else {3 + len(weights): 0},
        scratch_shapes=[
            pltpu.VMEM((pixels, lines), jnp.bfloat16),
            pltpu.VMEM((pixels, lines), jnp.bfloat16),
            pltpu.VMEM((pixels, 2 * elevations), jnp.float32),
            pltpu.VMEM((pixels, 2 * elevations), jnp.float32),
            pltpu.VMEM((2 * (elevations // tile_width), columns, tile_width), jnp.float32),
            pltpu.VMEM((2, columns, elevations), jnp.float32),
            pltpu.VMEM((BAND, columns, 2 * elevations), jnp.bfloat16),
            pltpu.SemaphoreType.DMA((BAND,)),
        ],
        compiler_params=pltpu.CompilerParams(vmem_limit_bytes=40 * 1024 * 1024),
        name="invert_apart" if apart else "invert_edge" if edge else "invert",
    )(active, targets, runs, *weights, *extra)


def place_kernel(last_ref, row_ref, last_row_ref, _, out_ref, sem):
    target = out_ref.at[out_ref.shape[0] - 1]

    @pl.when(last_ref[0] > 0)
    def _():
        copy = pltpu.make_async_copy(last_row_ref, target, sem)
        copy.start()
        copy.wait()

    @pl.when(last_ref[0] == 0)
    def _():
        copy = pltpu.make_async_copy(row_ref, target, sem)
        copy.start()
        copy.wait()


def place_last_row(is_last, row, last_row, out):
    far = pl.BlockSpec(memory_space=pl.ANY)
    whole = pl.BlockSpec(memory_space=pltpu.VMEM)
    return pl.pallas_call(
        place_kernel,
        in_specs=[pl.BlockSpec(memory_space=pltpu.SMEM), whole, whole, far],
        out_specs=far,
        out_shape=jax.ShapeDtypeStruct(out.shape, out.dtype),
        input_output_aliases={3: 0},
        scratch_shapes=[pltpu.SemaphoreType.DMA],
        compiler_params=pltpu.CompilerParams(vmem_limit_bytes=4 * 1024 * 1024),
        name="place_last_row",
    )(is_last, row, last_row, out)


def turned(value, step):
    count = lax.axis_size("acq")
    return lax.ppermute(value, "acq", [(i, (i + step) % count) for i in range(count)])


def steering_of(phase):
    scale = 1.0 / math.sqrt(phase.shape[1])
    real = (jnp.cos(phase) * scale).astype(jnp.bfloat16)
    imag = (jnp.sin(phase) * scale).astype(jnp.bfloat16)
    return jnp.concatenate([real, imag], axis=1)


def planes_of(steering, acqs):
    _, lines, elevations = steering.shape
    real, imag = steering[0, : lines // 2], steering[0, lines // 2 :]
    upper = jnp.concatenate([real, -imag], axis=1).reshape(-1, 1, acqs, 2 * elevations)
    lower = jnp.concatenate([imag, real], axis=1).reshape(-1, 1, acqs, 2 * elevations)
    plane = jnp.concatenate([upper, lower], axis=1).reshape(lines, 2 * elevations)
    return plane * STEP_SIZE, plane.T


def program(measurements, tile_order, steer_phase, group_ids):
    acqs = measurements.shape[0]
    rows, columns = group_ids.shape
    elevations = steer_phase.shape[2]
    assert rows % BAND == 0
    bands = rows // BAND
    edge = [rows - 1] + list(range(BAND - 1))
    inner = [list(range(BAND * b - 1, BAND * b + 2)) for b in range(1, bands)]
    early = 1
    spans = [edge + sum(inner[:early], []), sum(inner[early:], [])]
    sent = order_tiles(measurements, tile_order, spans, (rows - 1,))
    head = lax.all_to_all(sent[0], "acq", 0, 0, tiled=True)
    tail = lax.all_to_all(sent[1], "acq", 0, 0, tiled=True)
    mine = steering_of(steer_phase)
    before = turned(mine, 1)
    back, ahead = planes_of(mine, acqs)
    back_before, ahead_before = planes_of(before, acqs)
    runs = (group_ids % columns + BAND - 1) // BAND
    first = lax.axis_index("acq") == 0
    column = jnp.arange(columns, dtype=jnp.int32)
    turn = (columns - 1) % BAND
    last_starts = jnp.maximum(0, BAND * ((column - turn + BAND) // BAND) - BAND + turn)
    last_runs = (last_starts + BAND - 1) // BAND
    apart_runs = jnp.stack([last_runs, runs[0]])[None]
    inner_runs = runs[BAND - 1 : rows - 1 : BAND][:, None]
    count = lax.axis_size("acq")
    is_first = jnp.where(first, 1, 0).reshape(1)
    is_last = jnp.where(lax.axis_index("acq") == count - 1, 1, 0).reshape(1)
    shape = (rows, columns, 2 * elevations)
    sides = dict(offset=0, base=0, edge=True)
    both = [back_before, back], [ahead_before, ahead]
    out, above = invert(is_first, head, apart_runs, *both, shape, apart=True, **sides)
    last_row = lax.ppermute(above, "acq", [(0, count - 1)])
    out = invert(
        is_first, head, inner_runs[:early], [back], [ahead], shape, offset=1, base=1, out=out
    )
    out, above = invert(1 - is_first, head, runs[:1][None], *both, shape, out=out, **sides)
    row = lax.ppermute(above, "acq", [(i, i - 1) for i in range(1, count)])
    out = invert(
        is_first, tail, inner_runs[early:], [back], [ahead], shape,
        offset=0, base=1 + early, out=out,
    )
    return place_last_row(is_last, row, last_row, out)


def solution(mesh):
    placed = (
        P(("groups", "acq"), None, None, None, None),
        P("groups"),
        P(("groups", "acq"), None, None),
        P(("groups", "acq"), None),
    )
    return jax.shard_map(
        program,
        mesh=mesh,
        in_specs=placed,
        out_specs=P(("groups", "acq"), None, None),
        check_vma=False,
    )
```

```python
import functools
import math

import jax
import jax.numpy as jnp
from jax import lax
from jax.experimental import pallas as pl
from jax.experimental.pallas import tpu as pltpu
from jax.sharding import PartitionSpec as P


ITERS = 3
BAND = 3
STEP_SIZE = 0.0625
SHRINK_LEVEL = 3.0


def dot(a, b, dims=((1,), (0,))):
    return lax.dot_general(a, b, (dims, ((), ())), preferred_element_type=jnp.float32)


def order_kernel(order_ref, *refs, spans, ahead_rows):
    stack_ref, sent_refs = refs[0], refs[1:]
    acqs, parts, _, tiles, columns = stack_ref.shape
    lines = acqs * parts * tiles
    share = acqs * parts
    target = lax.broadcasted_iota(jnp.int32, (lines, 1), 0)
    source = lax.broadcasted_iota(jnp.int32, (1, lines), 1)
    block = lax.rem(source, tiles)
    part = lax.rem(lax.div(source, tiles), parts)
    acq = lax.div(source, tiles * parts)
    tile = jnp.zeros((1, lines), jnp.int32)
    for k in range(tiles):
        tile = jnp.where(block == k, order_ref[k], tile)
    after = jnp.where(tile == tiles - 1, 0, tile + 1)
    inner = part * acqs + acq
    pick = jnp.where(target == tile * share + inner, 1.0, 0.0).astype(jnp.bfloat16)
    pick_after = jnp.where(target == after * share + inner, 1.0, 0.0).astype(jnp.bfloat16)
    for sent_ref, span in zip(sent_refs, spans):
        for q, row in enumerate(span):
            lump = stack_ref[:, :, row].reshape(lines, columns)
            chosen = pick_after if row in ahead_rows else pick
            sent_ref[:, q * columns : (q + 1) * columns] = dot(chosen, lump).astype(sent_ref.dtype)


def order_tiles(measurements, tile_order, spans, ahead_rows):
    acqs, parts, tiles, _, columns = measurements.shape
    stack = measurements.transpose(0, 1, 3, 2, 4)
    lines = acqs * parts * tiles
    whole = pl.BlockSpec(memory_space=pltpu.VMEM)
    return pl.pallas_call(
        functools.partial(order_kernel, spans=spans, ahead_rows=ahead_rows),
        in_specs=[pl.BlockSpec(memory_space=pltpu.SMEM), whole],
        out_specs=[whole] * len(spans),
        out_shape=[
            jax.ShapeDtypeStruct((lines, len(span) * columns), measurements.dtype) for span in spans
        ],
        compiler_params=pltpu.CompilerParams(vmem_limit_bytes=8 * 1024 * 1024),
        name="order_tiles",
    )(tile_order, stack)


def run_sums(energy, pick):
    return dot(pick, energy.astype(jnp.bfloat16))


def shrink_factor(sums, pick):
    factor = jnp.maximum(1.0 - SHRINK_LEVEL * lax.rsqrt(jnp.maximum(sums, SHRINK_LEVEL**2)), 0.0)
    high = factor.astype(jnp.bfloat16)
    low = (factor - high.astype(jnp.float32)).astype(jnp.bfloat16)
    both = jnp.concatenate([high, low], axis=0)
    return dot(jnp.concatenate([pick, pick], axis=0), both, ((0,), (0,)))


def band_kernel(active_ref, *refs, edge, apart, base, held):
    settings = dict(edge=edge, apart=apart, base=base, held=held)
    if not edge:
        return band_body(*refs, **settings)

    @pl.when(active_ref[0] > 0)
    def _():
        band_body(*refs, **settings)


def band_body(target_ref, run_ref, *refs, edge, apart, base, held):
    refs = list(refs)
    back_refs = [refs.pop(0) for _ in range(2 if edge else 1)]
    ahead_refs = [refs.pop(0) for _ in range(2 if edge else 1)]
    if held:
        refs.pop(0)
    out_ref = refs.pop(0)
    above_ref = refs.pop(0) if edge else None
    target_sc, resid_sc, step_sc, past_sc, energy_sc, factor_sc, image_sc, sem = refs
    step = pl.program_id(0)
    steps = pl.num_programs(0)
    columns = run_ref.shape[2]
    elevations = factor_sc.shape[2]
    tile_width = energy_sc.shape[2]
    groups = -(-(columns // BAND + 2) // 16) * 16
    weight_of = (0,) + (len(back_refs) - 1,) * (BAND - 1)
    set_of = (0 if apart else 1,) + (1,) * (BAND - 1)
    span = [slice(q * columns, (q + 1) * columns) for q in range(BAND)]

    def copies(of):
        first = BAND * (base + of) - 1
        targets = [above_ref if edge and q == 0 else out_ref.at[first + q] for q in range(BAND)]
        return [pltpu.make_async_copy(image_sc.at[q], targets[q], sem.at[q]) for q in range(BAND)]

    group = lax.broadcasted_iota(jnp.int32, (groups, columns), 0)
    picks = [
        jnp.where(group == run_ref[0, n : n + 1], 1.0, 0.0).astype(jnp.bfloat16)
        for n in range(run_ref.shape[1])
    ]
    target_sc[...] = target_ref[...].T

    def descend(is_first):
        for at in range(0, elevations, tile_width):
            real = slice(at, at + tile_width)
            imag = slice(elevations + at, elevations + at + tile_width)
            for q in range(BAND):
                if is_first:
                    resid = target_sc[span[q]]
                else:
                    resid = resid_sc[span[q]]
                step_real = dot(resid, back_refs[weight_of[q]][:, real])
                step_imag = dot(resid, back_refs[weight_of[q]][:, imag])
                if not is_first:
                    step_real += past_sc[span[q], real]
                    step_imag += past_sc[span[q], imag]
                step_sc[span[q], real] = step_real
                step_sc[span[q], imag] = step_imag
                energy = step_real * step_real + step_imag * step_imag
                slot = 2 * (at // tile_width) + set_of[q]
                if q > 0 and set_of[q] == set_of[q - 1]:
                    energy += energy_sc[slot]
                energy_sc[slot] = energy

        for at in range(0, elevations, tile_width):
            real = slice(at, at + tile_width)
            slot = 2 * (at // tile_width)
            sums = run_sums(energy_sc[slot + 1], picks[-1])
            if apart:
                alone = run_sums(energy_sc[slot], picks[0])
                factor_sc[0, :, real] = shrink_factor(alone, picks[0])
            factor_sc[1, :, real] = shrink_factor(sums, picks[-1])

    def predict():
        for q in range(BAND):
            guess = jnp.zeros((columns, target_sc.shape[1]), jnp.float32)
            for half in range(2):
                part = slice(half * elevations, (half + 1) * elevations)
                settled = step_sc[span[q], part] * factor_sc[set_of[q]]
                past_sc[span[q], part] = settled
                guess += dot(settled.astype(jnp.bfloat16), ahead_refs[weight_of[q]][part])
            resid_sc[span[q]] = (target_sc[span[q]].astype(jnp.float32) - guess).astype(
                jnp.bfloat16
            )

    descend(True)

    @pl.loop(1, ITERS)
    def _(i):
        predict()
        descend(False)

    @pl.when(step > 0)
    def _():
        for copy in copies(step - 1):
            copy.wait()

    for q in range(BAND):
        for half in range(2):
            part = slice(half * elevations, (half + 1) * elevations)
            image_sc[q, :, part] = (step_sc[span[q], part] * factor_sc[set_of[q]]).astype(
                image_sc.dtype
            )
        copies(step)[q].start()

    @pl.when(step == steps - 1)
    def _():
        for copy in copies(step):
            copy.wait()


def invert(active, targets, runs, backs, aheads, out_shape, *, offset, base, edge=False, apart=False, out=None):
    lines = targets.shape[0]
    steps, kinds, columns = runs.shape
    elevations = backs[0].shape[1] // 2
    whole = pl.BlockSpec(memory_space=pltpu.VMEM)
    far = pl.BlockSpec(memory_space=pl.ANY)
    pixels = BAND * columns
    tile_width = 256
    shape = jax.ShapeDtypeStruct(out_shape, jnp.bfloat16)
    above = jax.ShapeDtypeStruct(out_shape[1:], jnp.bfloat16)
    weights = [*backs, *aheads]
    extra = [] if out is None else [out]
    return pl.pallas_call(
        functools.partial(
            band_kernel, edge=edge, apart=apart, base=base, held=out is not None
        ),
        grid=(steps,),
        in_specs=[
            pl.BlockSpec(memory_space=pltpu.SMEM),
            pl.BlockSpec((lines, pixels), lambda i: (0, i + offset)),
            pl.BlockSpec((1, kinds, columns), lambda i: (i, 0, 0)),
        ]
        + [whole] * len(weights)
        + [far] * len(extra),
        out_specs=[far, far] if edge else far,
        out_shape=[shape, above] if edge else shape,
        input_output_aliases={} if out is None else {3 + len(weights): 0},
        scratch_shapes=[
            pltpu.VMEM((pixels, lines), jnp.bfloat16),
            pltpu.VMEM((pixels, lines), jnp.bfloat16),
            pltpu.VMEM((pixels, 2 * elevations), jnp.float32),
            pltpu.VMEM((pixels, 2 * elevations), jnp.float32),
            pltpu.VMEM((2 * (elevations // tile_width), columns, tile_width), jnp.float32),
            pltpu.VMEM((2, columns, elevations), jnp.float32),
            pltpu.VMEM((BAND, columns, 2 * elevations), jnp.bfloat16),
            pltpu.SemaphoreType.DMA((BAND,)),
        ],
        compiler_params=pltpu.CompilerParams(vmem_limit_bytes=40 * 1024 * 1024),
        name="invert_apart" if apart else "invert_edge" if edge else "invert",
    )(active, targets, runs, *weights, *extra)


def place_kernel(last_ref, row_ref, last_row_ref, _, out_ref, sem):
    target = out_ref.at[out_ref.shape[0] - 1]

    @pl.when(last_ref[0] > 0)
    def _():
        copy = pltpu.make_async_copy(last_row_ref, target, sem)
        copy.start()
        copy.wait()

    @pl.when(last_ref[0] == 0)
    def _():
        copy = pltpu.make_async_copy(row_ref, target, sem)
        copy.start()
        copy.wait()


def place_last_row(is_last, row, last_row, out):
    far = pl.BlockSpec(memory_space=pl.ANY)
    whole = pl.BlockSpec(memory_space=pltpu.VMEM)
    return pl.pallas_call(
        place_kernel,
        in_specs=[pl.BlockSpec(memory_space=pltpu.SMEM), whole, whole, far],
        out_specs=far,
        out_shape=jax.ShapeDtypeStruct(out.shape, out.dtype),
        input_output_aliases={3: 0},
        scratch_shapes=[pltpu.SemaphoreType.DMA],
        compiler_params=pltpu.CompilerParams(vmem_limit_bytes=4 * 1024 * 1024),
        name="place_last_row",
    )(is_last, row, last_row, out)


def turned(value, step):
    count = lax.axis_size("acq")
    return lax.ppermute(value, "acq", [(i, (i + step) % count) for i in range(count)])


def steering_of(phase):
    scale = 1.0 / math.sqrt(phase.shape[1])
    real = (jnp.cos(phase) * scale).astype(jnp.bfloat16)
    imag = (jnp.sin(phase) * scale).astype(jnp.bfloat16)
    return jnp.concatenate([real, imag], axis=1)


def planes_of(steering, acqs):
    _, lines, elevations = steering.shape
    real, imag = steering[0, : lines // 2], steering[0, lines // 2 :]
    upper = jnp.concatenate([real, -imag], axis=1).reshape(-1, 1, acqs, 2 * elevations)
    lower = jnp.concatenate([imag, real], axis=1).reshape(-1, 1, acqs, 2 * elevations)
    plane = jnp.concatenate([upper, lower], axis=1).reshape(lines, 2 * elevations)
    return plane * STEP_SIZE, plane.T


def program(measurements, tile_order, steer_phase, group_ids):
    acqs = measurements.shape[0]
    rows, columns = group_ids.shape
    elevations = steer_phase.shape[2]
    assert rows % BAND == 0
    bands = rows // BAND
    edge = [rows - 1] + list(range(BAND - 1))
    inner = [list(range(BAND * b - 1, BAND * b + 2)) for b in range(1, bands)]
    early = 1
    spans = [edge + sum(inner[:early], []), sum(inner[early:], [])]
    sent = order_tiles(measurements, tile_order, spans, (rows - 1,))
    head = lax.all_to_all(sent[0], "acq", 0, 0, tiled=True)
    tail = lax.all_to_all(sent[1], "acq", 0, 0, tiled=True)
    mine = steering_of(steer_phase)
    before = turned(mine, 1)
    back, ahead = planes_of(mine, acqs)
    back_before, ahead_before = planes_of(before, acqs)
    runs = (group_ids % columns + BAND - 1) // BAND
    first = lax.axis_index("acq") == 0
    column = jnp.arange(columns, dtype=jnp.int32)
    turn = (columns - 1) % BAND
    last_starts = jnp.maximum(0, BAND * ((column - turn + BAND) // BAND) - BAND + turn)
    last_runs = (last_starts + BAND - 1) // BAND
    apart_runs = jnp.stack([last_runs, runs[0]])[None]
    inner_runs = runs[BAND - 1 : rows - 1 : BAND][:, None]
    count = lax.axis_size("acq")
    is_first = jnp.where(first, 1, 0).reshape(1)
    is_last = jnp.where(lax.axis_index("acq") == count - 1, 1, 0).reshape(1)
    shape = (rows, columns, 2 * elevations)
    out = invert(
        is_first, head, inner_runs[:early], [back], [ahead], shape, offset=1, base=1
    )
    sides = dict(offset=0, base=0, edge=True)
    both = [back_before, back], [ahead_before, ahead]
    out, above = invert(is_first, head, apart_runs, *both, shape, apart=True, out=out, **sides)
    last_row = lax.ppermute(above, "acq", [(0, count - 1)])
    out, above = invert(1 - is_first, head, runs[:1][None], *both, shape, out=out, **sides)
    row = lax.ppermute(above, "acq", [(i, i - 1) for i in range(1, count)])
    out = invert(
        is_first, tail, inner_runs[early:], [back], [ahead], shape,
        offset=0, base=1 + early, out=out,
    )
    return place_last_row(is_last, row, last_row, out)


def solution(mesh):
    placed = (
        P(("groups", "acq"), None, None, None, None),
        P("groups"),
        P(("groups", "acq"), None, None),
        P(("groups", "acq"), None),
    )
    return jax.shard_map(
        program,
        mesh=mesh,
        in_specs=placed,
        out_specs=P(("groups", "acq"), None, None),
        check_vma=False,
    )
```
